128 devices in a mesh: blk: 16 (over z, y_lo, core), lat: 8 (over x, y_hi).
Axes of the slice: x: 4, y: 4 (y_hi: 2, y_lo: 2; y = y_hi * 2 + y_lo), z: 4, core: 2. Of those that a mesh axis runs over, the one named last changes fastest.
Arguments:
- displacement: float32 [2, 3, 1272960], P(None, None, ('blk', 'lat')), may hold values from -5 to 5, as said below
- velocity: float32 [2, 3, 1272960], P(None, None, ('blk', 'lat')), may hold values from -2.5 to 2.5, as said below
- lumped_mass: float32 [1272960], P(('blk', 'lat')), may hold values from 0.25 to 225, as said below
- shear_modulus: float32 [125, 16384], P(None, ('blk', 'lat')), may hold values from 0.3 to 1
- lame_modulus: float32 [125, 16384], P(None, ('blk', 'lat')), may hold values from 0.3 to 1
- adjoint_sources: bfloat16 [32, 3, 1272960], P(None, None, ('blk', 'lat')), may hold values from -24 to 24
- node_numbers: int32 [125, 16384], P(None, ('blk', 'lat')), may hold values from 0 to 9944, as said below
- event_frequency: int32 [2, 32], replicated, may hold values from 0 to 31, each once within a row
Outputs:
- final_displacement: float32 [2, 3, 1272960], P(None, None, ('blk', 'lat'))
- final_velocity: float32 [2, 3, 1272960], P(None, None, ('blk', 'lat'))
- strain_spectrum: float32 [2, 32, 2, 5, 16384], P(None, None, None, None, ('blk', 'lat'))
The draws below stay inside these ranges and needn't reach their ends.
Inputs may be any that keep to these rules, and one draw needn't show every extreme that they name: `node_numbers`: each device's columns number its 9945 nodes, each node once across its elements' shared points. A device's element at grid place (ex, ey, ez), 0 <= ex < 2, 0 <= ey < 4, 0 <= ez < 16, touches a neighbour's face when ex or ey is at an end of its range; the first 128 columns of each device are these elements in the order of ex * 4 * 16 + ey * 16 + ez, the remaining columns the other elements in the same order. `event_frequency`: each row gives the events of one supershot distinct frequencies. `displacement`: all copies of a mesh node hold equal values. `velocity`: all copies of a mesh node hold equal values. `lumped_mass`: all copies of a mesh node hold equal values, the mass assembled over all elements of the mesh.
All inputs are finite; a program needn't handle non-finite values.
Results may differ from the reference program's by a relative error of at most 0.0034.
Values sent between devices are 32-bit elements; how exact they have to be, the bound alone decides.
No kernel may reach another device: no remote copies, remote signals or barrier semaphores. Data moves between devices by JAX's collectives and lax.ppermute only.
A program may use at most 128 MiB of HBM per device.

```python
import math
import jax
import jax.numpy as jnp
import numpy as np
from jax import lax

EXB = 2
EYL = 4
EZ = 16
SHOTS = 2
NFREQ = 32
STEP_TOTAL = 4
NODES_EL = 125
EVENTS = 32
NXN = 9
NYN = 17
NZN = 65
NODES_DEV = 9945
ELEMS = 128
FACE_B = 1105
FACE_L = 585
NODES = 1272960
ELEMS_ALL = 16384
N_BLK = 16
N_LAT = 8


def layout_tables(key):
    base = jax.random.fold_in(key, 4242)
    devices = N_BLK * N_LAT
    number_keys = jax.random.split(jax.random.fold_in(base, 1), devices)
    numbering = jax.vmap(lambda single: jax.random.permutation(single, NODES_DEV))(number_keys).astype(jnp.int32)
    elements = jnp.arange(ELEMS, dtype=jnp.int32)
    along = elements // (EYL * EZ)
    across = elements // EZ % EYL
    inner = ((along > 0) & (along < EXB - 1) & (across > 0) & (across < EYL - 1)).astype(jnp.int32)
    scores = inner * ELEMS + elements
    single_order = jnp.argsort(scores).astype(jnp.int32)
    order = jnp.broadcast_to(single_order[None, :], (devices, ELEMS))
    return (numbering, order)


def global_index(numbering):
    devices = N_BLK * N_LAT
    cycle_span = N_BLK * (NXN - 1)
    lat_span = N_LAT * (NYN - 1) + 1
    device_ids = jnp.arange(devices, dtype=jnp.int32)
    cycle_pos = device_ids // N_LAT
    lat_pos = device_ids % N_LAT
    local = jnp.arange(NODES_DEV, dtype=jnp.int32)
    first = local // (NYN * NZN)
    second = local // NZN % NYN
    third = local % NZN
    cycle_coord = (cycle_pos[:, None] * (NXN - 1) + first[None, :]) % cycle_span
    lat_coord = lat_pos[:, None] * (NYN - 1) + second[None, :]
    structured = (cycle_coord * lat_span + lat_coord) * NZN + third[None, :]
    inverse = jnp.argsort(numbering, axis=1).astype(jnp.int32)
    return jnp.take_along_axis(structured, inverse, axis=1).reshape(-1)


def grid_total():
    return N_BLK * (NXN - 1) * (N_LAT * (NYN - 1) + 1) * NZN


def draw_displacement(key, part):
    numbering, order = layout_tables(key)
    noise_key = jax.random.fold_in(key, 11)
    values = jnp.clip(jax.random.normal(noise_key, (SHOTS * 3, grid_total()), jnp.float32), -5.0, 5.0)
    return values[:, global_index(numbering)].reshape(SHOTS, 3, -1)


def draw_velocity(key, part):
    numbering, order = layout_tables(key)
    noise_key = jax.random.fold_in(key, 12)
    values = jnp.clip(0.5 * jax.random.normal(noise_key, (SHOTS * 3, grid_total()), jnp.float32), -2.5, 2.5)
    return values[:, global_index(numbering)].reshape(SHOTS, 3, -1)


def assembled_weights(span, closed):
    table = jnp.array([0.2, 49.0 / 90.0, 32.0 / 45.0, 49.0 / 90.0], jnp.float32)
    coords = jnp.arange(span, dtype=jnp.int32)
    values = table[coords % 4]
    if closed:
        return values
    ends = (coords == 0) | (coords == span - 1)
    return jnp.where(ends, 0.1, values)


def draw_lumped_mass(key, part):
    numbering, order = layout_tables(key)
    noise_key = jax.random.fold_in(key, 13)
    cycle_span = N_BLK * (NXN - 1)
    lat_span = N_LAT * (NYN - 1) + 1
    density = jnp.exp(jax.random.uniform(noise_key, (grid_total(),), jnp.float32, jnp.log(2000.0), jnp.log(5000.0)))
    cube = assembled_weights(cycle_span, True)[:, None, None] * assembled_weights(lat_span, False)[None, :, None] * assembled_weights(NZN, False)[None, None, :] / 8.0
    mass = density * cube.reshape(-1)
    return mass[global_index(numbering)]


def draw_node_numbers(key, part):
    numbering, order = layout_tables(key)
    along = order // (EYL * EZ)
    across = order // EZ % EYL
    depth = order % EZ
    points = jnp.arange(125, dtype=jnp.int32)
    first = points // 25
    second = points // 5 % 5
    third = points % 5
    grid = ((4 * along[:, None, :] + first[None, :, None]) * NYN + 4 * across[:, None, :] + second[None, :, None]) * NZN + 4 * depth[:, None, :] + third[None, :, None]
    numbers = jax.vmap(lambda table, where: table[where])(numbering, grid)
    return numbers.transpose(1, 0, 2).reshape(125, -1).astype(jnp.int32)


def shard_levels(key, shape, shards, low, top_value):
    factor_of = 1.0
    for position, parts in shards:
        heights = jax.random.uniform(jax.random.fold_in(jax.random.fold_in(key, 6), position), (parts,), jnp.float32, low / len(shards), top_value / len(shards))
        factor_of = factor_of * jnp.repeat(jnp.exp(heights), shape[position] // parts).reshape((-1,) + (1,) * (len(shape) - 1 - position))
    return factor_of


def centred(key, extent, deviation, most, cuts=(), kind=jnp.bfloat16):
    values = jax.random.normal(key, extent, jnp.float32) * deviation
    if len(cuts) > 0:
        values = shard_levels(key, extent, cuts, -0.22, 0.18) * values
    return jnp.clip(values, min=-most, max=most).astype(kind)


def setup_inputs(seed: int = 0) -> dict:
    key_of = jax.random.split(jax.random.key(seed), 9)
    return {
        "displacement": draw_displacement(jax.random.fold_in(key_of[8], 71), 0),
        "velocity": draw_velocity(jax.random.fold_in(key_of[8], 71), 0),
        "lumped_mass": draw_lumped_mass(jax.random.fold_in(key_of[8], 71), 0),
        "shear_modulus": jnp.clip(jnp.exp(math.log(1.0) - 1.2039728 * jax.random.uniform(key_of[3], (NODES_EL, ELEMS_ALL), jnp.float32) ** shard_levels(key_of[3], (NODES_EL, ELEMS_ALL), ((1, 128),), -0.2, 0.2)), 0.3, 1.0),
        "lame_modulus": jnp.clip(jnp.exp(math.log(1.0) - 1.2039728 * jax.random.uniform(key_of[4], (NODES_EL, ELEMS_ALL), jnp.float32) ** shard_levels(key_of[4], (NODES_EL, ELEMS_ALL), ((1, 128),), -0.2, 0.2)), 0.3, 1.0),
        "adjoint_sources": centred(key_of[5], (EVENTS, 3, NODES), 4.0, 24.0, ((2, 128),)),
        "node_numbers": draw_node_numbers(jax.random.fold_in(key_of[8], 71), 0),
        "event_frequency": jax.vmap(lambda own: jax.random.permutation(own, NFREQ))(jax.random.split(key_of[7], SHOTS)).reshape((SHOTS, NFREQ)).astype(jnp.int32),
    }


highest = lax.Precision.HIGHEST

def gll_tables():
    points = np.array([-1.0, -math.sqrt(3.0 / 7.0), 0.0, math.sqrt(3.0 / 7.0), 1.0])
    weights = np.array([0.1, 49.0 / 90.0, 32.0 / 45.0, 49.0 / 90.0, 0.1])
    products = np.ones(5)
    for target in range(5):
        for source in range(5):
            if source != target:
                products[target] = products[target] * (points[target] - points[source])
    derivative = np.zeros((5, 5))
    for target in range(5):
        for source in range(5):
            if source != target:
                derivative[target, source] = products[target] / products[source] / (points[target] - points[source])
        derivative[target, target] = -np.sum(derivative[target])
    weight_cube = weights[:, None, None] * weights[None, :, None] * weights[None, None, :] / 8.0
    return (jnp.asarray(derivative, jnp.float32), jnp.asarray(weight_cube, jnp.float32))

def grid_tables():
    elements = np.arange(ELEMS)
    along = elements // (EYL * EZ)
    across = elements // EZ % EYL
    inner = ((along > 0) & (along < EXB - 1) & (across > 0) & (across < EYL - 1)).astype(np.int64)
    order = np.argsort(inner * ELEMS + elements, kind='stable')
    columns_of = np.argsort(order, kind='stable')
    nodes = np.arange(NODES_DEV)
    first = nodes // (NYN * NZN)
    second = nodes // NZN % NYN
    third = nodes % NZN
    elem_x = np.minimum(first // 4, EXB - 1)
    elem_y = np.minimum(second // 4, EYL - 1)
    elem_z = np.minimum(third // 4, EZ - 1)
    point_rows = 25 * (first - 4 * elem_x) + 5 * (second - 4 * elem_y) + (third - 4 * elem_z)
    point_cols = columns_of[(elem_x * EYL + elem_y) * EZ + elem_z]
    return (order, columns_of, point_rows, point_cols)

def face_places():
    span_b = np.arange(NYN * NZN)
    cycle_low = span_b
    cycle_high = (NXN - 1) * NYN * NZN + span_b
    span_l = np.arange(NXN * NZN)
    rows = span_l // NZN
    deep = span_l % NZN
    lat_low = rows * NYN * NZN + deep
    lat_high = (rows * NYN + NYN - 1) * NZN + deep
    return (np.stack([cycle_low, cycle_high]), np.stack([lat_low, lat_high]))

def source_terms(event_frequency):
    angular_frequencies = jnp.pi * (1.0 + jnp.arange(NFREQ, dtype=jnp.float32)) / (NFREQ + 1.0)
    onehot = (event_frequency[:, :, None] == jnp.arange(NFREQ, dtype=jnp.int32)[None, None, :]).astype(jnp.float32)
    selected_entry = lax.optimization_barrier(jnp.sum(onehot * angular_frequencies[None, None, :], axis=2))
    sample_times = 1.0 + jnp.arange(STEP_TOTAL, dtype=jnp.float32)
    source_pulse = jnp.cos(sample_times[:, None, None] * selected_entry[None, :, :])
    phase_angles = angular_frequencies[:, None] * sample_times[None, :]
    spectra = jnp.stack([jnp.cos(phase_angles), -jnp.sin(phase_angles)])
    return (source_pulse.astype(jnp.bfloat16), spectra)

def element_forces(motion, numbers, shear, lame, derivative, weight_cube):
    elem_count = numbers.shape[1]
    shot_count = motion.shape[0] // 3
    nodal = motion[:, numbers].reshape(shot_count, 3, 5, 5, 5, elem_count)
    grads = (2.0 * jnp.einsum('il,scljkn->scijkn', derivative, nodal, precision=highest), 2.0 * jnp.einsum('jl,scilkn->scijkn', derivative, nodal, precision=highest), 2.0 * jnp.einsum('kl,scijln->scijkn', derivative, nodal, precision=highest))
    shear_pts = shear.reshape(5, 5, 5, elem_count)
    lame_pts = lame.reshape(5, 5, 5, elem_count)
    trace = grads[0][:, 0] + grads[1][:, 1] + grads[2][:, 2]
    pressure = lame_pts * trace
    weighted = weight_cube[:, :, :, None]
    forms = ('il,scijkn->scljkn', 'jl,scijkn->scilkn', 'kl,scijkn->scijln')
    internal = jnp.zeros(nodal.shape, jnp.float32)
    for direction in range(3):
        pieces = []
        for strain_part in range(3):
            stress = shear_pts * (grads[direction][:, strain_part] + grads[strain_part][:, direction])
            if strain_part == direction:
                stress = stress + pressure
            pieces.append(weighted * stress)
        flux = jnp.stack(pieces, axis=1)
        internal = internal + jnp.einsum(forms[direction], derivative, flux, precision=highest)
    internal = 2.0 * internal.reshape(3 * shot_count, 125, elem_count)
    summed = jnp.zeros(motion.shape, jnp.float32).at[:, numbers].add(internal)
    third = trace / 3.0
    strains = jnp.stack([grads[0][:, 0] - third, grads[1][:, 1] - third, 0.5 * (grads[0][:, 1] + grads[1][:, 0]), 0.5 * (grads[0][:, 2] + grads[2][:, 0]), 0.5 * (grads[1][:, 2] + grads[2][:, 1])], axis=1)
    integral = jnp.einsum('sqijkn,ijk->sqn', strains, weight_cube, precision=highest)
    return (summed, integral)

def pick_faces(values, index):
    return values[:, index]

def place_faces(values, index, extra):
    return values.at[:, index].add(extra)

def assemble(balance, cycle_index, lat_index):
    devices = N_BLK * N_LAT
    components = balance.shape[1]
    pick = jax.vmap(pick_faces)
    place = jax.vmap(place_faces)
    cycle_vals = pick(balance, cycle_index).reshape(N_BLK, N_LAT, components, 2, FACE_B)
    from_lower = jnp.roll(cycle_vals[:, :, :, 1], 1, axis=0).reshape(devices, components, FACE_B)
    from_upper = jnp.roll(cycle_vals[:, :, :, 0], -1, axis=0).reshape(devices, components, FACE_B)
    balance = place(balance, cycle_index[:, 0], from_lower)
    balance = place(balance, cycle_index[:, 1], from_upper)
    lat_vals = pick(balance, lat_index).reshape(N_BLK, N_LAT, components, 2, FACE_L)
    zero_row = jnp.zeros_like(lat_vals[:, :1, :, 1])
    from_lower = jnp.concatenate([zero_row, lat_vals[:, :-1, :, 1]], axis=1).reshape(devices, components, FACE_L)
    from_upper = jnp.concatenate([lat_vals[:, 1:, :, 0], zero_row], axis=1).reshape(devices, components, FACE_L)
    balance = place(balance, lat_index[:, 0], from_lower)
    balance = place(balance, lat_index[:, 1], from_upper)
    return balance

def reference(displacement, velocity, lumped_mass, shear_modulus, lame_modulus, adjoint_sources, node_numbers, event_frequency):
    devices = N_BLK * N_LAT
    components = 3 * SHOTS
    node_count = displacement.shape[2] // devices
    elem_count = node_numbers.shape[1] // devices
    derivative, weight_cube = gll_tables()
    source_pulse, spectra = source_terms(event_frequency)
    order, columns_of, point_rows, point_cols = grid_tables()
    cycle_place, lat_place = face_places()

    def split(array, width):
        return array.reshape(array.shape[0], devices, width).transpose(1, 0, 2)
    motion = split(displacement.reshape(components, -1), node_count)
    speeds = split(velocity.reshape(components, -1), node_count)
    masses = lumped_mass.reshape(devices, 1, node_count)
    numbers = split(node_numbers, elem_count)
    shear_dev = split(shear_modulus, elem_count)
    lame_dev = split(lame_modulus, elem_count)
    grid_nodes = numbers[:, point_rows, point_cols]
    cycle_index = grid_nodes[:, cycle_place]
    lat_index = grid_nodes[:, lat_place]
    flat_sources = adjoint_sources.reshape(adjoint_sources.shape[0], -1)
    spectrum = jnp.zeros((2, NFREQ, SHOTS, 5, devices, elem_count), jnp.float32)

    def local_work(inputs):
        return element_forces(inputs[0], inputs[1], inputs[2], inputs[3], derivative, weight_cube)
    for step in range(STEP_TOTAL):
        force = jnp.dot(source_pulse[step], flat_sources, preferred_element_type=jnp.float32)
        force = split(force.reshape(components, -1), node_count)
        internal, integral = lax.map(local_work, (motion, numbers, shear_dev, lame_dev))
        balance = assemble(force - internal, cycle_index, lat_index)
        speeds = speeds + balance / masses
        spectrum = spectrum + spectra[:, :, step][:, :, None, None, None, None] * integral.transpose(1, 2, 0, 3)[None, None]
        motion = motion + speeds
    final_displacement = motion.transpose(1, 0, 2).reshape(SHOTS, 3, devices * node_count)
    final_velocity = speeds.transpose(1, 0, 2).reshape(SHOTS, 3, devices * node_count)
    return (final_displacement, final_velocity, spectrum.reshape(2, NFREQ, SHOTS, 5, devices * elem_count))
```

```python
import math

import jax
import jax.numpy as jnp
import numpy as np
from jax import lax
from jax.experimental import pallas as pl
from jax.experimental.pallas import tpu as pltpu
from jax.sharding import PartitionSpec as P

EXB = 2
EYL = 4
EZ = 16
NFREQ = 32
EVENTS = 32
STEP_TOTAL = 4
NXN = 9
NYN = 17
NZN = 65
NODES_DEV = 9945
NODE_BLOCKS = 78
LINE = 72
COMPS = 40


bf16 = jnp.bfloat16
f32 = jnp.float32


def gll_numpy():
    points = np.array([-1.0, -math.sqrt(3.0 / 7.0), 0.0, math.sqrt(3.0 / 7.0), 1.0])
    weights = np.array([0.1, 49.0 / 90.0, 32.0 / 45.0, 49.0 / 90.0, 0.1])
    products = np.ones(5)
    for target in range(5):
        for source in range(5):
            if source != target:
                products[target] *= points[target] - points[source]
    derivative = np.zeros((5, 5))
    for target in range(5):
        for source in range(5):
            if source != target:
                derivative[target, source] = (
                    products[target] / products[source] / (points[target] - points[source])
                )
        derivative[target, target] = -np.sum(derivative[target])
    cube = weights[:, None, None] * weights[None, :, None] * weights[None, None, :] / 8.0
    return derivative, cube.reshape(125)


def split_np(matrix):
    high = np.asarray(matrix, np.float32).astype(bf16)
    low = (matrix - high.astype(np.float64)).astype(np.float32).astype(bf16)
    return high, low


def operator_tables():
    derivative, cube = gll_numpy()
    eye = np.eye(5)
    parts = [
        2.0 * np.kron(np.kron(derivative, eye), eye),
        2.0 * np.kron(np.kron(eye, derivative), eye),
        2.0 * np.kron(np.kron(eye, eye), derivative),
    ]
    forward = np.zeros((3, 128, 128))
    backward = np.zeros((128, 3, 128))
    for d in range(3):
        forward[d, :125, :125] = parts[d]
        forward[d, 125, :125] = cube @ parts[d]
        backward[:125, d, :125] = parts[d].T
    fwd_high, fwd_low = split_np(forward.reshape(384, 128))
    bwd_high, bwd_low = split_np(backward.reshape(128, 384))
    gradient = np.concatenate([fwd_high, fwd_high, fwd_low], axis=1)
    divergence = np.concatenate([bwd_high, bwd_high, bwd_low], axis=1)
    weight = np.zeros((128, 128), np.float32)
    weight[:125] = cube[:, None]
    return gradient, divergence, weight


def frequency_tables():
    omega = np.pi * (1.0 + np.arange(NFREQ)) / (NFREQ + 1.0)
    times = 1.0 + np.arange(STEP_TOTAL)
    angles = omega[:, None] * times[None, :]
    pulses = np.cos(angles).astype(np.float32).T
    spectra = np.concatenate([np.cos(angles), -np.sin(angles)], axis=0)
    wide = np.einsum("rk,mn->rmkn", spectra, np.eye(10)).reshape(64 * 10, STEP_TOTAL * 10)
    high, low = split_np(wide)
    zero = np.zeros((640, 8), high.dtype)
    return pulses, np.concatenate([high, high, low, zero], axis=1)


def split2(values):
    high = values.astype(bf16)
    low = (values - high.astype(f32)).astype(bf16)
    return high, low


def vmem():
    return pl.BlockSpec(memory_space=pltpu.VMEM)


def smem():
    return pl.BlockSpec(memory_space=pltpu.SMEM)


def line_place(line):
    ix = line // NYN
    iy = line - ix * NYN
    ex = jnp.minimum(ix // 4, EXB - 1)
    ey = jnp.minimum(iy // 4, EYL - 1)
    row = 25 * (ix - 4 * ex) + 5 * (iy - 4 * ey)
    col = 64 * ex + 16 * ey
    return row, col


def gather_kernel(
    numbers,
    mixing,
    sources,
    displacement,
    velocity,
    mass,
    shear,
    lame,
    weight,
    force_out,
    motion_out,
    speed_out,
    inverse_out,
    shear_out,
    lame_out,
    rows,
    table,
    lines,
):
    flat = sources[...].reshape(3 * EVENTS, NODES_DEV)
    rows[0:24, 0:NODES_DEV] = jnp.dot(mixing[...], flat, preferred_element_type=f32)
    for q in range(3):
        rows[24 + 2 * q : 26 + 2 * q, 0:NODES_DEV] = displacement[q]
        rows[32 + 2 * q : 34 + 2 * q, 0:NODES_DEV] = velocity[q]
    rows[38:39, 0:NODES_DEV] = mass[...]

    def transpose_block(block, carry):
        start = pl.multiple_of(block * 128, 128)
        table[pl.ds(start, 128), 0:COMPS] = rows[:, pl.ds(start, 128)].T
        return carry

    lax.fori_loop(0, NODE_BLOCKS, transpose_block, 0)

    def gather_line(line, carry):
        row, col = line_place(line)
        for z in range(NZN):
            ez = min(z // 4, EZ - 1)
            node = numbers[row + (z - 4 * ez), col + ez]
            lines[pl.ds(line * LINE + z, 1), :] = table[pl.ds(node, 1), :]
        return carry

    lax.fori_loop(0, NXN * NYN, gather_line, 0)

    def element_rows(pair, carry):
        a = pair // 5
        b = pair - 5 * a
        for c in range(5):
            pieces = []
            for ex in range(EXB):
                for ey in range(EYL):
                    line = (4 * ex + a) * NYN + 4 * ey + b
                    pieces.append(lines[pl.ds(line * LINE + c, EZ, stride=4), :])
            turned = jnp.concatenate(pieces, axis=0).T
            point = pair * 5 + c
            force_out[pl.ds(point, 24, stride=128), :] = turned[0:24]
            motion_out[pl.ds(point, 6, stride=128), :] = turned[24:30]
            speed_out[pl.ds(point, 6, stride=128), :] = turned[32:38]
            inverse_out[pl.ds(point, 1), :] = 1.0 / turned[38:39]
        return carry

    lax.fori_loop(0, 25, element_rows, 0)
    for point in range(125, 128):
        force_out[pl.ds(point, 24, stride=128), :] = jnp.zeros((24, 128), f32)
        motion_out[pl.ds(point, 6, stride=128), :] = jnp.zeros((6, 128), f32)
        speed_out[pl.ds(point, 6, stride=128), :] = jnp.zeros((6, 128), f32)
    inverse_out[125:128, :] = jnp.zeros((3, 128), f32)
    shear_out[0:125, :] = shear[...] * weight[0:125, :]
    shear_out[125:128, :] = jnp.zeros((3, 128), f32)
    lame_out[0:125, :] = lame[...] * weight[0:125, :]
    lame_out[125:128, :] = jnp.zeros((3, 128), f32)


def lanes_of(count):
    return lax.broadcasted_iota(jnp.int32, (count, 128), 1)


def balance_of(motion, force, step, shear, lame, gradient, divergence, balance, integral):
    fields = jnp.concatenate([motion[128 * j : 128 * j + 128, :] for j in range(6)], axis=1)
    high, low = split2(fields)
    grads = jnp.dot(
        gradient[...], jnp.concatenate([high, low, high], axis=0), preferred_element_type=f32
    )

    def grad(d, q, s):
        j = 2 * q + s
        return grads[128 * d : 128 * d + 128, 128 * j : 128 * j + 128]

    mu = shear[...]
    lam = lame[...]
    stress = {}
    for s in range(2):
        pressure = lam * (grad(0, 0, s) + grad(1, 1, s) + grad(2, 2, s))
        for d in range(3):
            for q in range(d, 3):
                value = mu * (grad(d, q, s) + grad(q, d, s))
                if q == d:
                    value = value + pressure
                stress[d, q, s] = stress[q, d, s] = split2(value)
    highs, lows = (
        jnp.concatenate(
            [
                jnp.concatenate([stress[d, j // 2, j % 2][part] for j in range(6)], axis=1)
                for d in range(3)
            ],
            axis=0,
        )
        for part in range(2)
    )
    internal = jnp.dot(
        divergence[...], jnp.concatenate([highs, lows, highs], axis=0), preferred_element_type=f32
    )
    for j in range(6):
        balance[128 * j : 128 * j + 128, :] = internal[:, 128 * j : 128 * j + 128]

    def weighted(d, q):
        row = 128 * d + 125
        return jnp.concatenate(
            [grads[row : row + 1, 128 * j : 128 * j + 128] for j in (2 * q, 2 * q + 1)], axis=0
        )

    third = (weighted(0, 0) + weighted(1, 1) + weighted(2, 2)) / 3.0
    integral[0:2, :] = weighted(0, 0) - third
    integral[2:4, :] = weighted(1, 1) - third
    integral[4:6, :] = 0.5 * (weighted(0, 1) + weighted(1, 0))
    integral[6:8, :] = 0.5 * (weighted(0, 2) + weighted(2, 0))
    integral[8:10, :] = 0.5 * (weighted(1, 2) + weighted(2, 1))

    lane = lanes_of(25)
    keep = lane % 16
    for j in range(6):
        base = 128 * j
        first = balance[pl.ds(base, 25, stride=5), :]
        last = balance[pl.ds(base + 4, 25, stride=5), :]
        balance[pl.ds(base, 25, stride=5), :] = first + jnp.where(
            keep != 0, pltpu.roll(last, 1, 1), 0.0
        )
        balance[pl.ds(base + 4, 25, stride=5), :] = last + jnp.where(
            keep != 15, pltpu.roll(first, 127, 1), 0.0
        )
    side = lanes_of(5) % 64
    for j in range(6):
        for a in range(5):
            base = 128 * j + 25 * a
            first = balance[base : base + 5, :]
            last = balance[base + 20 : base + 25, :]
            balance[base : base + 5, :] = first + jnp.where(
                side >= 16, pltpu.roll(last, 16, 1), 0.0
            )
            balance[base + 20 : base + 25, :] = last + jnp.where(
                side < 48, pltpu.roll(first, 112, 1), 0.0
            )
    for j in range(6):
        base = 128 * j
        first = balance[base : base + 25, :]
        last = balance[base + 100 : base + 125, :]
        balance[base : base + 25, :] = first + jnp.where(
            lane >= 64, pltpu.roll(last, 64, 1), 0.0
        )
        balance[base + 100 : base + 125, :] = last + jnp.where(
            lane < 64, pltpu.roll(first, 64, 1), 0.0
        )
    balance[...] = force[768 * step : 768 * step + 768, :] - balance[...]


def pack_cycle(balance, place, even_out, odd_out):
    lane = lanes_of(25)
    even = place[0] == 0
    for g in range(3):
        near, far = 128 * g, 128 * (g + 3)
        low = jnp.where(
            lane < 64, balance[near : near + 25, :], pltpu.roll(balance[far : far + 25, :], 64, 1)
        )
        up = jnp.where(
            lane < 64,
            pltpu.roll(balance[near + 100 : near + 125, :], 64, 1),
            balance[far + 100 : far + 125, :],
        )
        even_out[32 * g : 32 * g + 25, :] = jnp.where(even, up, low)
        odd_out[32 * g : 32 * g + 25, :] = jnp.where(even, low, up)


def add_cycle(balance, place, even_in, odd_in):
    lane = lanes_of(25)
    even = place[0] == 0
    for g in range(3):
        near, far = 128 * g, 128 * (g + 3)
        first = even_in[32 * g : 32 * g + 25, :]
        second = odd_in[32 * g : 32 * g + 25, :]
        up = jnp.where(even, first, second)
        low = jnp.where(even, second, first)
        balance[near : near + 25, :] += jnp.where(lane < 64, low, 0.0)
        balance[far : far + 25, :] += jnp.where(lane < 64, pltpu.roll(low, 64, 1), 0.0)
        balance[near + 100 : near + 125, :] += jnp.where(lane >= 64, pltpu.roll(up, 64, 1), 0.0)
        balance[far + 100 : far + 125, :] += jnp.where(lane >= 64, up, 0.0)


def turn(values, slots):
    return values if slots % 8 == 0 else pltpu.roll(values, (16 * slots) % 128, 1)


def pack_lat(balance, place, even_out, odd_out):
    slot = lanes_of(5) // 16 % 4
    even = place[1] == 0
    for g in range(2):
        for a in range(5):
            low = jnp.zeros((5, 128), f32)
            up = jnp.zeros((5, 128), f32)
            for t in range(4):
                j = 4 * g + t
                if j >= 6:
                    break
                base = 128 * j + 25 * a
                low = jnp.where(slot == t, turn(balance[base : base + 5, :], t), low)
                up = jnp.where(slot == t, turn(balance[base + 20 : base + 25, :], t - 3), up)
            at = 32 * g + 5 * a
            even_out[at : at + 5, :] = jnp.where(even, up, low)
            odd_out[at : at + 5, :] = jnp.where(even, low, up)


def add_lat(balance, place, even_in, odd_in):
    slot = lanes_of(5) // 16 % 4
    even = place[1] == 0
    for g in range(2):
        for a in range(5):
            at = 32 * g + 5 * a
            first = even_in[at : at + 5, :]
            second = odd_in[at : at + 5, :]
            up = jnp.where(even, first, second)
            low = jnp.where(even, second, first)
            for t in range(4):
                j = 4 * g + t
                if j >= 6:
                    break
                base = 128 * j + 25 * a
                balance[base : base + 5, :] += jnp.where(slot == 0, turn(low, -t), 0.0)
                balance[base + 20 : base + 25, :] += jnp.where(slot == 3, turn(up, 3 - t), 0.0)


def first_kernel(
    place, motion, force, shear, lame, gradient, divergence, balance, integral, even_out, odd_out
):
    balance_of(motion, force, 0, shear, lame, gradient, divergence, balance, integral)
    pack_cycle(balance, place, even_out, odd_out)


def middle_kernel(place, old, even_in, odd_in, balance, even_out, odd_out):
    balance[...] = old[...]
    add_cycle(balance, place, even_in, odd_in)
    pack_lat(balance, place, even_out, odd_out)


def advance(place, old, even_in, odd_in, inverse, motion_in, speed_in, motion, speed, balance):
    balance[...] = old[...]
    add_lat(balance, place, even_in, odd_in)
    scale = inverse[...]
    for j in range(6):
        part = slice(128 * j, 128 * j + 128)
        now = speed_in[part, :] + balance[part, :] * scale
        speed[part, :] = now
        motion[part, :] = motion_in[part, :] + now


def make_step_kernel(step):
    def step_kernel(
        place,
        old,
        even_in,
        odd_in,
        inverse,
        motion_in,
        speed_in,
        force,
        shear,
        lame,
        gradient,
        divergence,
        balance,
        motion,
        speed,
        integral,
        even_out,
        odd_out,
    ):
        advance(place, old, even_in, odd_in, inverse, motion_in, speed_in, motion, speed, balance)
        balance_of(motion, force, step, shear, lame, gradient, divergence, balance, integral)
        pack_cycle(balance, place, even_out, odd_out)

    return step_kernel


def last_kernel(
    numbers,
    place,
    old,
    even_in,
    odd_in,
    inverse,
    motion_in,
    speed_in,
    motion_out,
    speed_out,
    balance,
    state,
    points,
    table,
):
    advance(
        place,
        old,
        even_in,
        odd_in,
        inverse,
        motion_in,
        speed_in,
        state.at[0:768, :],
        state.at[768:1536, :],
        balance,
    )

    def point_rows(point, carry):
        values = state[pl.ds(point, 12, stride=128), :]
        values = jnp.concatenate([values, jnp.zeros((4, 128), f32)], axis=0)
        start = pl.multiple_of(point * 128, 128)
        points[pl.ds(start, 128), 0:16] = values.T
        return carry

    lax.fori_loop(0, 125, point_rows, 0)

    def scatter_line(line, carry):
        row, col = line_place(line)
        start = row * 128 + col
        for z in range(NZN):
            ez = min(z // 4, EZ - 1)
            c = z - 4 * ez
            node = numbers[row + c, col + ez]
            table[pl.ds(node, 1), :] = points[pl.ds(start + 128 * c + ez, 1), :]
        return carry

    lax.fori_loop(0, NXN * NYN, scatter_line, 0)

    def turned(start):
        return table[pl.ds(start, 128), :].T

    def transpose_block(block, carry):
        start = pl.multiple_of(block * 128, 128)
        values = turned(start)
        for q in range(3):
            motion_out[q, :, pl.ds(start, 128)] = values[2 * q : 2 * q + 2]
            speed_out[q, :, pl.ds(start, 128)] = values[6 + 2 * q : 8 + 2 * q]
        return carry

    lax.fori_loop(0, NODE_BLOCKS - 1, transpose_block, 0)
    start = 128 * (NODE_BLOCKS - 1)
    rest = NODES_DEV - start
    values = turned(start)
    for q in range(3):
        motion_out[q, :, start:NODES_DEV] = values[2 * q : 2 * q + 2, 0:rest]
        speed_out[q, :, start:NODES_DEV] = values[6 + 2 * q : 8 + 2 * q, 0:rest]


def spectrum_kernel(wide, first, second, third, fourth, out):
    values = jnp.concatenate([part[...] for part in (first, second, third, fourth)], axis=0)
    high, low = split2(values)
    zero = jnp.zeros((8, 128), bf16)
    out[...] = jnp.dot(
        wide[...], jnp.concatenate([high, low, high, zero], axis=0), preferred_element_type=f32
    )


def shape(*extent):
    return jax.ShapeDtypeStruct(extent, f32)


def local(
    displacement,
    velocity,
    lumped_mass,
    shear_modulus,
    lame_modulus,
    adjoint_sources,
    node_numbers,
    event_frequency,
):
    gradient, divergence, weight = (jnp.asarray(table) for table in operator_tables())
    pulses, wide = frequency_tables()
    onehot = (event_frequency[:, :, None] == jnp.arange(NFREQ, dtype=jnp.int32)).astype(f32)
    wavelet = jnp.sum(onehot[None] * jnp.asarray(pulses)[:, None, None, :], axis=-1)
    mixing = (
        jnp.eye(3, dtype=f32)[None, :, None, :, None] * wavelet[:, None, :, None, :]
    ).reshape(24, 3 * EVENTS).astype(bf16)
    blk = lax.axis_index("blk")
    lat = lax.axis_index("lat")
    place = jnp.stack([blk % 2, lat % 2]).astype(jnp.int32)
    blk_count = lax.axis_size("blk")
    lat_count = lax.axis_size("lat")
    cycle_even = [(i, i ^ 1) for i in range(blk_count)]
    cycle_odd = [(i, (((i + 1) ^ 1) - 1) % blk_count) for i in range(blk_count)]
    lat_even = [(i, i ^ 1) for i in range(lat_count)]
    lat_odd = [(i, ((i + 1) ^ 1) - 1) for i in range(1, lat_count - 1)]

    force, motion, speed, inverse, shear, lame = pl.pallas_call(
        gather_kernel,
        out_shape=(
            shape(24 * 128, 128),
            shape(768, 128),
            shape(768, 128),
            shape(128, 128),
            shape(128, 128),
            shape(128, 128),
        ),
        in_specs=[smem()] + [vmem()] * 8,
        out_specs=[vmem()] * 6,
        scratch_shapes=[
            pltpu.VMEM((COMPS, NODE_BLOCKS * 128), f32),
            pltpu.VMEM((NODE_BLOCKS * 128, 128), f32),
            pltpu.VMEM((NXN * NYN * LINE, 128), f32),
        ],
        name="gather",
    )(
        node_numbers,
        mixing,
        adjoint_sources.transpose(1, 0, 2),
        displacement.transpose(1, 0, 2),
        velocity.transpose(1, 0, 2),
        lumped_mass.reshape(1, NODES_DEV),
        shear_modulus,
        lame_modulus,
        weight,
    )
    balance_shape, integral_shape = shape(768, 128), shape(10, 128)
    cycle_shape, lat_shape = shape(96, 128), shape(64, 128)
    integrals = []
    for step in range(STEP_TOTAL):
        if step == 0:
            balance, integral, even, odd = pl.pallas_call(
                first_kernel,
                out_shape=(balance_shape, integral_shape, cycle_shape, cycle_shape),
                in_specs=[smem()] + [vmem()] * 6,
                out_specs=[vmem()] * 4,
                name="first",
            )(place, motion, force, shear, lame, gradient, divergence)
        else:
            balance, motion, speed, integral, even, odd = pl.pallas_call(
                make_step_kernel(step),
                out_shape=(
                    balance_shape,
                    balance_shape,
                    balance_shape,
                    integral_shape,
                    cycle_shape,
                    cycle_shape,
                ),
                in_specs=[smem()] + [vmem()] * 11,
                out_specs=[vmem()] * 6,
                name="step",
            )(
                place,
                balance,
                even,
                odd,
                inverse,
                motion,
                speed,
                force,
                shear,
                lame,
                gradient,
                divergence,
            )
        integrals.append(integral)
        odd = lax.ppermute(odd, "blk", cycle_odd)
        even = lax.ppermute(even, "blk", cycle_even)
        balance, even, odd = pl.pallas_call(
            middle_kernel,
            out_shape=(balance_shape, lat_shape, lat_shape),
            in_specs=[smem()] + [vmem()] * 3,
            out_specs=[vmem()] * 3,
            name="middle",
        )(place, balance, even, odd)
        odd = lax.ppermute(odd, "lat", lat_odd)
        even = lax.ppermute(even, "lat", lat_even)
    spectrum = pl.pallas_call(
        spectrum_kernel,
        out_shape=shape(640, 128),
        in_specs=[vmem()] * 5,
        out_specs=vmem(),
        name="spectrum",
    )(jnp.asarray(wide), *integrals)
    final_motion, final_speed = pl.pallas_call(
        last_kernel,
        out_shape=(shape(3, 2, NODES_DEV), shape(3, 2, NODES_DEV)),
        in_specs=[smem()] * 2 + [vmem()] * 6,
        out_specs=[vmem()] * 2,
        scratch_shapes=[
            pltpu.VMEM((768, 128), f32),
            pltpu.VMEM((1536, 128), f32),
            pltpu.VMEM((125 * 128, 128), f32),
            pltpu.VMEM((NODE_BLOCKS * 128, 128), f32),
        ],
        name="last",
    )(node_numbers, place, balance, even, odd, inverse, motion, speed)
    return (
        final_motion.transpose(1, 0, 2),
        final_speed.transpose(1, 0, 2),
        spectrum.reshape(2, NFREQ, 5, 2, 128).transpose(0, 1, 3, 2, 4),
    )


def solution(mesh):
    nodes = P(None, None, ("blk", "lat"))
    columns = P(None, ("blk", "lat"))
    return jax.shard_map(
        local,
        mesh=mesh,
        in_specs=(nodes, nodes, P(("blk", "lat")), columns, columns, nodes, columns, P()),
        out_specs=(nodes, nodes, P(None, None, None, None, ("blk", "lat"))),
        check_vma=False,
    )
```

```python
import math

import jax
import jax.numpy as jnp
import numpy as np
from jax import lax
from jax.experimental import pallas as pl
from jax.experimental.pallas import tpu as pltpu
from jax.sharding import PartitionSpec as P

EXB = 2
EYL = 4
EZ = 16
NFREQ = 32
EVENTS = 32
STEP_TOTAL = 4
NXN = 9
NYN = 17
NZN = 65
NODES_DEV = 9945
NODE_BLOCKS = 78
LINE = 72
COMPS = 40


bf16 = jnp.bfloat16
f32 = jnp.float32


def gll_numpy():
    points = np.array([-1.0, -math.sqrt(3.0 / 7.0), 0.0, math.sqrt(3.0 / 7.0), 1.0])
    weights = np.array([0.1, 49.0 / 90.0, 32.0 / 45.0, 49.0 / 90.0, 0.1])
    products = np.ones(5)
    for target in range(5):
        for source in range(5):
            if source != target:
                products[target] *= points[target] - points[source]
    derivative = np.zeros((5, 5))
    for target in range(5):
        for source in range(5):
            if source != target:
                derivative[target, source] = (
                    products[target] / products[source] / (points[target] - points[source])
                )
        derivative[target, target] = -np.sum(derivative[target])
    cube = weights[:, None, None] * weights[None, :, None] * weights[None, None, :] / 8.0
    return derivative, cube.reshape(125)


def split_np(matrix):
    high = np.asarray(matrix, np.float32).astype(bf16)
    low = (matrix - high.astype(np.float64)).astype(np.float32).astype(bf16)
    return high, low


def operator_tables():
    derivative, cube = gll_numpy()
    eye = np.eye(5)
    parts = [
        2.0 * np.kron(np.kron(derivative, eye), eye),
        2.0 * np.kron(np.kron(eye, derivative), eye),
        2.0 * np.kron(np.kron(eye, eye), derivative),
    ]
    forward = np.zeros((3, 128, 128))
    backward = np.zeros((128, 3, 128))
    for d in range(3):
        forward[d, :125, :125] = parts[d]
        forward[d, 125, :125] = cube @ parts[d]
        backward[:125, d, :125] = parts[d].T
    fwd_high, fwd_low = split_np(forward.reshape(384, 128))
    bwd_high, bwd_low = split_np(backward.reshape(128, 384))
    gradient = np.concatenate([fwd_high, fwd_high, fwd_low], axis=1)
    divergence = np.concatenate([bwd_high, bwd_high, bwd_low], axis=1)
    weight = np.zeros((128, 128), np.float32)
    weight[:125] = cube[:, None]
    return gradient, divergence, weight


def frequency_tables():
    omega = np.pi * (1.0 + np.arange(NFREQ)) / (NFREQ + 1.0)
    times = 1.0 + np.arange(STEP_TOTAL)
    angles = omega[:, None] * times[None, :]
    pulses = np.zeros((8, NFREQ), np.float32)
    pulses[:STEP_TOTAL] = np.cos(angles).T
    pulses = pulses.astype(bf16)
    spectra = np.concatenate([np.cos(angles), -np.sin(angles)], axis=0)
    wide = np.einsum("rk,mn->rmkn", spectra, np.eye(10)).reshape(64 * 10, STEP_TOTAL * 10)
    high, low = split_np(wide)
    zero = np.zeros((640, 8), high.dtype)
    return pulses, np.concatenate([high, high, low, zero], axis=1)


def split2(values):
    high = values.astype(bf16)
    low = (values - high.astype(f32)).astype(bf16)
    return high, low


def vmem():
    return pl.BlockSpec(memory_space=pltpu.VMEM)


def smem():
    return pl.BlockSpec(memory_space=pltpu.SMEM)


def for_lines(body):
    def plane(ix, carry):
        ex = jnp.minimum(lax.shift_right_logical(ix, 2), EXB - 1)
        plane_start = 3200 * (ix - 4 * ex) + 64 * ex

        def line(iy, inner):
            ey = jnp.minimum(lax.shift_right_logical(iy, 2), EYL - 1)
            body(ix * NYN + iy, plane_start + 640 * (iy - 4 * ey) + 16 * ey)
            return inner

        return lax.fori_loop(0, NYN, line, carry)

    lax.fori_loop(0, NXN, plane, 0)


def line_offset(z):
    ez = min(z // 4, EZ - 1)
    return 128 * (z - 4 * ez) + ez


def for_blocks(count, unroll, body):
    def group(index, carry):
        for part in range(unroll):
            body(index * unroll + part)
        return carry

    lax.fori_loop(0, count // unroll, group, 0)


def gather_kernel(
    numbers_hbm,
    sources_hbm,
    displacement_hbm,
    velocity_hbm,
    mass_hbm,
    shear_hbm,
    lame_hbm,
    weight_hbm,
    pulses_hbm,
    frequency_hbm,
    force_out,
    motion_out,
    speed_out,
    inverse_out,
    shear_out,
    lame_out,
    mixing,
    rows,
    table,
    lines,
    numbers,
    sources,
    displacement,
    velocity,
    mass,
    shear,
    lame,
    weight,
    pulses,
    frequency,
    sems,
):
    copies = [
        pltpu.make_async_copy(source, target, sems.at[position])
        for position, (source, target) in enumerate(
            (
                (frequency_hbm, frequency),
                (pulses_hbm, pulses),
                (sources_hbm, sources),
                (displacement_hbm, displacement),
                (velocity_hbm, velocity),
                (mass_hbm, mass),
                (numbers_hbm, numbers),
                (shear_hbm, shear),
                (lame_hbm, lame),
                (weight_hbm, weight),
            )
        )
    ]
    for copy in copies:
        copy.start()
    for copy in copies[0:2]:
        copy.wait()
    index = lax.broadcasted_iota(jnp.int32, (NFREQ, EVENTS), 0)
    mixing[...] = jnp.zeros((24, 3 * EVENTS), f32)
    for s in range(2):
        chosen = (frequency[s : s + 1, :] == index).astype(f32).astype(bf16)
        wavelet = jnp.dot(pulses[...], chosen, preferred_element_type=f32)
        for k in range(STEP_TOTAL):
            for q in range(3):
                row = 6 * k + 2 * q + s
                mixing[row : row + 1, EVENTS * q : EVENTS * (q + 1)] = wavelet[k : k + 1]
    for copy in copies[3:6]:
        copy.wait()
    for q in range(3):
        rows[24 + 2 * q : 26 + 2 * q, 0:NODES_DEV] = displacement[q]
        rows[32 + 2 * q : 34 + 2 * q, 0:NODES_DEV] = velocity[q]
    rows[38:39, 0:NODES_DEV] = mass[...].reshape(1, NODES_DEV)
    copies[2].wait()
    flat = sources[...].reshape(3 * EVENTS, NODES_DEV)
    rows[0:24, 0:NODES_DEV] = jnp.dot(
        mixing[...].astype(bf16), flat, preferred_element_type=f32
    )

    def transpose_block(block):
        start = pl.multiple_of(block * 128, 128)
        table[pl.ds(start, 128), 0:COMPS] = rows[:, pl.ds(start, 128)].T

    for_blocks(NODE_BLOCKS, 6, transpose_block)
    for copy in copies[6:]:
        copy.wait()

    def gather_line(line, start):
        for z in range(NZN):
            node = numbers[start + line_offset(z)]
            lines[pl.ds(line * LINE + z, 1), :] = table[pl.ds(node, 1), :]

    for_lines(gather_line)

    def element_rows(pair):
        a = lax.shift_right_logical(pair * 13, 6)
        b = pair - 5 * a
        for c in range(5):
            pieces = []
            for ex in range(EXB):
                for ey in range(EYL):
                    line = (4 * ex + a) * NYN + 4 * ey + b
                    pieces.append(lines[pl.ds(line * LINE + c, EZ, stride=4), :])
            turned = jnp.concatenate(pieces, axis=0).T
            point = pair * 5 + c
            force_out[pl.ds(point, 24, stride=128), :] = turned[0:24]
            motion_out[pl.ds(point, 6, stride=128), :] = turned[24:30]
            speed_out[pl.ds(point, 6, stride=128), :] = turned[32:38]
            inverse_out[pl.ds(point, 1), :] = 1.0 / turned[38:39]

    for_blocks(25, 1, element_rows)
    for point in range(125, 128):
        force_out[pl.ds(point, 24, stride=128), :] = jnp.zeros((24, 128), f32)
        motion_out[pl.ds(point, 6, stride=128), :] = jnp.zeros((6, 128), f32)
        speed_out[pl.ds(point, 6, stride=128), :] = jnp.zeros((6, 128), f32)
    inverse_out[125:128, :] = jnp.zeros((3, 128), f32)
    shear_out[0:125, :] = shear[...] * weight[0:125, :]
    shear_out[125:128, :] = jnp.zeros((3, 128), f32)
    lame_out[0:125, :] = lame[...] * weight[0:125, :]
    lame_out[125:128, :] = jnp.zeros((3, 128), f32)


def lanes_of(count):
    return lax.broadcasted_iota(jnp.int32, (count, 128), 1)


def balance_of(motion, force, step, shear, lame, gradient, divergence, balance, integral):
    fields = jnp.concatenate([motion[128 * j : 128 * j + 128, :] for j in range(6)], axis=1)
    high, low = split2(fields)
    grads = jnp.dot(
        gradient[...], jnp.concatenate([high, low, high], axis=0), preferred_element_type=f32
    )

    def grad(d, q, s):
        j = 2 * q + s
        return grads[128 * d : 128 * d + 128, 128 * j : 128 * j + 128]

    mu = shear[...]
    lam = lame[...]
    stress = {}
    for s in range(2):
        pressure = lam * (grad(0, 0, s) + grad(1, 1, s) + grad(2, 2, s))
        for d in range(3):
            for q in range(d, 3):
                value = mu * (grad(d, q, s) + grad(q, d, s))
                if q == d:
                    value = value + pressure
                stress[d, q, s] = stress[q, d, s] = split2(value)
    highs, lows = (
        jnp.concatenate(
            [
                jnp.concatenate([stress[d, j // 2, j % 2][part] for j in range(6)], axis=1)
                for d in range(3)
            ],
            axis=0,
        )
        for part in range(2)
    )
    internal = jnp.dot(
        divergence[...], jnp.concatenate([highs, lows, highs], axis=0), preferred_element_type=f32
    )
    for j in range(6):
        balance[128 * j : 128 * j + 128, :] = internal[:, 128 * j : 128 * j + 128]

    def weighted(d, q):
        row = 128 * d + 125
        return jnp.concatenate(
            [grads[row : row + 1, 128 * j : 128 * j + 128] for j in (2 * q, 2 * q + 1)], axis=0
        )

    third = (weighted(0, 0) + weighted(1, 1) + weighted(2, 2)) / 3.0
    integral[0:2, :] = weighted(0, 0) - third
    integral[2:4, :] = weighted(1, 1) - third
    integral[4:6, :] = 0.5 * (weighted(0, 1) + weighted(1, 0))
    integral[6:8, :] = 0.5 * (weighted(0, 2) + weighted(2, 0))
    integral[8:10, :] = 0.5 * (weighted(1, 2) + weighted(2, 1))

    lane = lanes_of(25)
    keep = lane % 16
    for j in range(6):
        base = 128 * j
        first = balance[pl.ds(base, 25, stride=5), :]
        last = balance[pl.ds(base + 4, 25, stride=5), :]
        balance[pl.ds(base, 25, stride=5), :] = first + jnp.where(
            keep != 0, pltpu.roll(last, 1, 1), 0.0
        )
        balance[pl.ds(base + 4, 25, stride=5), :] = last + jnp.where(
            keep != 15, pltpu.roll(first, 127, 1), 0.0
        )
    side = lanes_of(5) % 64
    for j in range(6):
        for a in range(5):
            base = 128 * j + 25 * a
            first = balance[base : base + 5, :]
            last = balance[base + 20 : base + 25, :]
            balance[base : base + 5, :] = first + jnp.where(
                side >= 16, pltpu.roll(last, 16, 1), 0.0
            )
            balance[base + 20 : base + 25, :] = last + jnp.where(
                side < 48, pltpu.roll(first, 112, 1), 0.0
            )
    for j in range(6):
        base = 128 * j
        first = balance[base : base + 25, :]
        last = balance[base + 100 : base + 125, :]
        balance[base : base + 25, :] = first + jnp.where(
            lane >= 64, pltpu.roll(last, 64, 1), 0.0
        )
        balance[base + 100 : base + 125, :] = last + jnp.where(
            lane < 64, pltpu.roll(first, 64, 1), 0.0
        )
    balance[...] = force[768 * step : 768 * step + 768, :] - balance[...]


def pack_cycle(balance, side, even_out, odd_out):
    lane = lanes_of(25)
    even = (side[0] & 1) == 0
    for g in range(3):
        near, far = 128 * g, 128 * (g + 3)
        low = jnp.where(
            lane < 64, balance[near : near + 25, :], pltpu.roll(balance[far : far + 25, :], 64, 1)
        )
        up = jnp.where(
            lane < 64,
            pltpu.roll(balance[near + 100 : near + 125, :], 64, 1),
            balance[far + 100 : far + 125, :],
        )
        even_out[32 * g : 32 * g + 25, :] = jnp.where(even, up, low)
        odd_out[32 * g : 32 * g + 25, :] = jnp.where(even, low, up)


def add_cycle(balance, side, even_in, odd_in):
    lane = lanes_of(25)
    even = (side[0] & 1) == 0
    for g in range(3):
        near, far = 128 * g, 128 * (g + 3)
        first = even_in[32 * g : 32 * g + 25, :]
        second = odd_in[32 * g : 32 * g + 25, :]
        up = jnp.where(even, first, second)
        low = jnp.where(even, second, first)
        balance[near : near + 25, :] += jnp.where(lane < 64, low, 0.0)
        balance[far : far + 25, :] += jnp.where(lane < 64, pltpu.roll(low, 64, 1), 0.0)
        balance[near + 100 : near + 125, :] += jnp.where(lane >= 64, pltpu.roll(up, 64, 1), 0.0)
        balance[far + 100 : far + 125, :] += jnp.where(lane >= 64, up, 0.0)


def turn(values, slots):
    return values if slots % 8 == 0 else pltpu.roll(values, (16 * slots) % 128, 1)


def pack_lat(balance, side, even_out, odd_out):
    slot = lanes_of(5) // 16 % 4
    even = (side[0] & 1) == 0
    for g in range(2):
        for a in range(5):
            low = jnp.zeros((5, 128), f32)
            up = jnp.zeros((5, 128), f32)
            for t in range(4):
                j = 4 * g + t
                if j >= 6:
                    break
                base = 128 * j + 25 * a
                low = jnp.where(slot == t, turn(balance[base : base + 5, :], t), low)
                up = jnp.where(slot == t, turn(balance[base + 20 : base + 25, :], t - 3), up)
            at = 32 * g + 5 * a
            even_out[at : at + 5, :] = jnp.where(even, up, low)
            odd_out[at : at + 5, :] = jnp.where(even, low, up)


def add_lat(balance, side, even_in, odd_in):
    slot = lanes_of(5) // 16 % 4
    even = (side[0] & 1) == 0
    for g in range(2):
        for a in range(5):
            at = 32 * g + 5 * a
            first = even_in[at : at + 5, :]
            second = odd_in[at : at + 5, :]
            up = jnp.where(even, first, second)
            low = jnp.where(even, second, first)
            for t in range(4):
                j = 4 * g + t
                if j >= 6:
                    break
                base = 128 * j + 25 * a
                balance[base : base + 5, :] += jnp.where(slot == 0, turn(low, -t), 0.0)
                balance[base + 20 : base + 25, :] += jnp.where(slot == 3, turn(up, 3 - t), 0.0)


def first_kernel(
    blk, motion, force, shear, lame, gradient, divergence, balance, integral, even_out, odd_out
):
    balance_of(motion, force, 0, shear, lame, gradient, divergence, balance, integral)
    pack_cycle(balance, blk, even_out, odd_out)


def middle_kernel(blk, lat, old, even_in, odd_in, balance, even_out, odd_out):
    balance[...] = old[...]
    add_cycle(balance, blk, even_in, odd_in)
    pack_lat(balance, lat, even_out, odd_out)


def advance(lat, old, even_in, odd_in, inverse, motion_in, speed_in, motion, speed, balance):
    balance[...] = old[...]
    add_lat(balance, lat, even_in, odd_in)
    scale = inverse[...]
    for j in range(6):
        part = slice(128 * j, 128 * j + 128)
        now = speed_in[part, :] + balance[part, :] * scale
        speed[part, :] = now
        motion[part, :] = motion_in[part, :] + now


def make_step_kernel(step):
    def step_kernel(
        blk,
        lat,
        old,
        even_in,
        odd_in,
        inverse,
        motion_in,
        speed_in,
        force,
        shear,
        lame,
        gradient,
        divergence,
        balance,
        motion,
        speed,
        integral,
        even_out,
        odd_out,
    ):
        advance(lat, old, even_in, odd_in, inverse, motion_in, speed_in, motion, speed, balance)
        balance_of(motion, force, step, shear, lame, gradient, divergence, balance, integral)
        pack_cycle(balance, blk, even_out, odd_out)

    return step_kernel


def last_kernel(
    numbers,
    lat,
    old,
    even_in,
    odd_in,
    inverse,
    motion_in,
    speed_in,
    motion_out,
    speed_out,
    balance,
    state,
    points,
    table,
):
    advance(
        lat,
        old,
        even_in,
        odd_in,
        inverse,
        motion_in,
        speed_in,
        state.at[0:768, :],
        state.at[768:1536, :],
        balance,
    )

    def point_rows(point):
        values = state[pl.ds(point, 12, stride=128), :]
        values = jnp.concatenate([values, jnp.zeros((4, 128), f32)], axis=0)
        start = pl.multiple_of(point * 128, 128)
        points[pl.ds(start, 128), 0:16] = values.T

    for_blocks(125, 5, point_rows)

    def scatter_line(line, start):
        del line
        for z in range(NZN):
            node = numbers[start + line_offset(z)]
            table[pl.ds(node, 1), :] = points[pl.ds(start + line_offset(z), 1), :]

    for_lines(scatter_line)

    def turned(start):
        return table[pl.ds(start, 128), :].T

    def transpose_block(block):
        start = pl.multiple_of(block * 128, 128)
        values = turned(start)
        for q in range(3):
            motion_out[q, :, pl.ds(start, 128)] = values[2 * q : 2 * q + 2]
            speed_out[q, :, pl.ds(start, 128)] = values[6 + 2 * q : 8 + 2 * q]

    for_blocks(NODE_BLOCKS - 1, 7, transpose_block)
    start = 128 * (NODE_BLOCKS - 1)
    rest = NODES_DEV - start
    values = turned(start)
    for q in range(3):
        motion_out[q, :, start:NODES_DEV] = values[2 * q : 2 * q + 2, 0:rest]
        speed_out[q, :, start:NODES_DEV] = values[6 + 2 * q : 8 + 2 * q, 0:rest]


def spectrum_kernel(wide, first, second, third, fourth, out):
    values = jnp.concatenate([part[...] for part in (first, second, third, fourth)], axis=0)
    high, low = split2(values)
    zero = jnp.zeros((8, 128), bf16)
    out[...] = jnp.dot(
        wide[...], jnp.concatenate([high, low, high, zero], axis=0), preferred_element_type=f32
    )


def kept(*extent):
    return pltpu.VMEM(extent, f32)


def hold(*arrays):
    return tuple(pltpu.with_memory_space_constraint(array, pltpu.VMEM) for array in arrays)


def limit(mebibytes):
    return pltpu.CompilerParams(vmem_limit_bytes=mebibytes * 1024 * 1024)


def local(
    displacement,
    velocity,
    lumped_mass,
    shear_modulus,
    lame_modulus,
    adjoint_sources,
    node_numbers,
    event_frequency,
):
    gradient, divergence, weight = (jnp.asarray(table) for table in operator_tables())
    pulses, wide = frequency_tables()
    blk = lax.axis_index("blk").astype(jnp.int32).reshape(1)
    lat = lax.axis_index("lat").astype(jnp.int32).reshape(1)
    numbers = node_numbers.reshape(125 * 128)
    blk_count = lax.axis_size("blk")
    lat_count = lax.axis_size("lat")
    cycle_even = [(i, i ^ 1) for i in range(blk_count)]
    cycle_odd = [(i, (((i + 1) ^ 1) - 1) % blk_count) for i in range(blk_count)]
    lat_even = [(i, i ^ 1) for i in range(lat_count)]
    lat_odd = [(i, ((i + 1) ^ 1) - 1) for i in range(1, lat_count - 1)]

    force, motion, speed, inverse, shear, lame = pl.pallas_call(
        gather_kernel,
        out_shape=(
            kept(24 * 128, 128),
            kept(768, 128),
            kept(768, 128),
            kept(128, 128),
            kept(128, 128),
            kept(128, 128),
        ),
        in_specs=[pl.BlockSpec(memory_space=pltpu.HBM)] * 10,
        out_specs=[vmem()] * 6,
        scratch_shapes=[
            pltpu.VMEM((24, 3 * EVENTS), f32),
            pltpu.VMEM((COMPS, NODE_BLOCKS * 128), f32),
            pltpu.VMEM((NODE_BLOCKS * 128, 128), f32),
            pltpu.VMEM((NXN * NYN * LINE, 128), f32),
            pltpu.SMEM((125 * 128,), jnp.int32),
            pltpu.VMEM((3, EVENTS, NODES_DEV), bf16),
            pltpu.VMEM((3, 2, NODES_DEV), f32),
            pltpu.VMEM((3, 2, NODES_DEV), f32),
            pltpu.VMEM((NODES_DEV,), f32),
            pltpu.VMEM((125, 128), f32),
            pltpu.VMEM((125, 128), f32),
            pltpu.VMEM((128, 128), f32),
            pltpu.VMEM((8, NFREQ), bf16),
            pltpu.VMEM((2, EVENTS), jnp.int32),
            pltpu.SemaphoreType.DMA((10,)),
        ],
        compiler_params=limit(24),
        name="gather",
    )(
        *(
            pltpu.with_memory_space_constraint(array, pltpu.HBM)
            for array in (
                numbers,
                adjoint_sources.transpose(1, 0, 2),
                displacement.transpose(1, 0, 2),
                velocity.transpose(1, 0, 2),
                lumped_mass,
                shear_modulus,
                lame_modulus,
                weight,
                jnp.asarray(pulses),
                event_frequency,
            )
        )
    )
    force, motion, speed, inverse, shear, lame, gradient, divergence = hold(
        force, motion, speed, inverse, shear, lame, gradient, divergence
    )
    balance_shape, integral_shape = kept(768, 128), kept(10, 128)
    cycle_shape, lat_shape = kept(96, 128), kept(64, 128)
    integrals = []
    for step in range(STEP_TOTAL):
        if step == 0:
            balance, integral, even, odd = pl.pallas_call(
                first_kernel,
                out_shape=(balance_shape, integral_shape, cycle_shape, cycle_shape),
                in_specs=[smem()] + [vmem()] * 6,
                out_specs=[vmem()] * 4,
                compiler_params=limit(8),
                name="first",
            )(blk, motion, force, shear, lame, gradient, divergence)
        else:
            balance, motion, speed, integral, even, odd = pl.pallas_call(
                make_step_kernel(step),
                out_shape=(
                    balance_shape,
                    balance_shape,
                    balance_shape,
                    integral_shape,
                    cycle_shape,
                    cycle_shape,
                ),
                in_specs=[smem()] * 2 + [vmem()] * 11,
                out_specs=[vmem()] * 6,
                compiler_params=limit(8),
                name="step",
            )(
                blk,
                lat,
                balance,
                even,
                odd,
                inverse,
                motion,
                speed,
                force,
                shear,
                lame,
                gradient,
                divergence,
            )
            motion, speed = hold(motion, speed)
        integrals.append(integral)
        odd = lax.ppermute(odd, "blk", cycle_odd)
        even = lax.ppermute(even, "blk", cycle_even)
        balance, even, odd = pl.pallas_call(
            middle_kernel,
            out_shape=(balance_shape, lat_shape, lat_shape),
            in_specs=[smem()] * 2 + [vmem()] * 3,
            out_specs=[vmem()] * 3,
            compiler_params=limit(8),
            name="middle",
        )(blk, lat, *hold(balance, even, odd))
        odd = lax.ppermute(odd, "lat", lat_odd)
        even = lax.ppermute(even, "lat", lat_even)
        balance, even, odd = hold(balance, even, odd)
    spectrum = pl.pallas_call(
        spectrum_kernel,
        out_shape=jax.ShapeDtypeStruct((640, 128), f32),
        in_specs=[vmem()] * 5,
        out_specs=vmem(),
        compiler_params=limit(8),
        name="spectrum",
    )(*hold(jnp.asarray(wide), *integrals))
    nodal = jax.ShapeDtypeStruct((3, 2, NODES_DEV), f32)
    final_motion, final_speed = pl.pallas_call(
        last_kernel,
        out_shape=(nodal, nodal),
        in_specs=[smem()] * 2 + [vmem()] * 6,
        out_specs=[vmem()] * 2,
        scratch_shapes=[
            pltpu.VMEM((768, 128), f32),
            pltpu.VMEM((1536, 128), f32),
            pltpu.VMEM((125 * 128, 128), f32),
            pltpu.VMEM((NODE_BLOCKS * 128, 128), f32),
        ],
        compiler_params=limit(24),
        name="last",
    )(numbers, lat, balance, even, odd, inverse, motion, speed)
    return (
        final_motion.transpose(1, 0, 2),
        final_speed.transpose(1, 0, 2),
        spectrum.reshape(2, NFREQ, 5, 2, 128).transpose(0, 1, 3, 2, 4),
    )


def solution(mesh):
    nodes = P(None, None, ("blk", "lat"))
    columns = P(None, ("blk", "lat"))
    return jax.shard_map(
        local,
        mesh=mesh,
        in_specs=(nodes, nodes, P(("blk", "lat")), columns, columns, nodes, columns, P()),
        out_specs=(nodes, nodes, P(None, None, None, None, ("blk", "lat"))),
        check_vma=False,
    )
```

```python
import math

import jax
import jax.numpy as jnp
import numpy as np
from jax import lax
from jax.experimental import pallas as pl
from jax.experimental.pallas import tpu as pltpu
from jax.sharding import PartitionSpec as P


EXB = 2
EYL = 4
EZ = 16
NFREQ = 32
EVENTS = 32
STEP_TOTAL = 4
NXN = 9
NYN = 17
NODES_DEV = 9945
NODE_BLOCKS = 78
LINE = 72
COMPS = 40
SLOTS = 4


bf16 = jnp.bfloat16
f32 = jnp.float32


def gll_numpy():
    points = np.array([-1.0, -math.sqrt(3.0 / 7.0), 0.0, math.sqrt(3.0 / 7.0), 1.0])
    weights = np.array([0.1, 49.0 / 90.0, 32.0 / 45.0, 49.0 / 90.0, 0.1])
    products = np.ones(5)
    for target in range(5):
        for source in range(5):
            if source != target:
                products[target] *= points[target] - points[source]
    derivative = np.zeros((5, 5))
    for target in range(5):
        for source in range(5):
            if source != target:
                derivative[target, source] = (
                    products[target] / products[source] / (points[target] - points[source])
                )
        derivative[target, target] = -np.sum(derivative[target])
    cube = weights[:, None, None] * weights[None, :, None] * weights[None, None, :] / 8.0
    return derivative, cube.reshape(125)


def split_np(matrix):
    high = np.asarray(matrix, np.float32).astype(bf16)
    low = (matrix - high.astype(np.float64)).astype(np.float32).astype(bf16)
    return high, low


def operator_tables():
    derivative, cube = gll_numpy()
    eye = np.eye(5)
    parts = [
        2.0 * np.kron(np.kron(derivative, eye), eye),
        2.0 * np.kron(np.kron(eye, derivative), eye),
        2.0 * np.kron(np.kron(eye, eye), derivative),
    ]
    forward = np.zeros((3, 128, 128))
    backward = np.zeros((128, 3, 128))
    for d in range(3):
        forward[d, :125, :125] = parts[d]
        forward[d, 125, :125] = cube @ parts[d]
        backward[:125, d, :125] = parts[d].T
    fwd_high, fwd_low = split_np(forward.reshape(384, 128))
    bwd_high, bwd_low = split_np(backward.reshape(128, 384))
    gradient = np.concatenate([fwd_high, fwd_high, fwd_low], axis=1)
    divergence = np.concatenate([bwd_high, bwd_high, bwd_low], axis=1)
    weight = np.zeros((128, 128), np.float32)
    weight[:125] = cube[:, None]
    return gradient, divergence, weight


def frequency_tables():
    omega = np.pi * (1.0 + np.arange(NFREQ)) / (NFREQ + 1.0)
    times = 1.0 + np.arange(STEP_TOTAL)
    angles = omega[:, None] * times[None, :]
    pulses = np.zeros((8, NFREQ), np.float32)
    pulses[:STEP_TOTAL] = np.cos(angles).T
    pulses = pulses.astype(bf16)
    spectra = np.concatenate([np.cos(angles), -np.sin(angles)], axis=0)
    wide = np.einsum("rk,mn->rmkn", spectra, np.eye(10)).reshape(64 * 10, STEP_TOTAL * 10)
    high, low = split_np(wide)
    zero = np.zeros((640, 8), high.dtype)
    return pulses, np.concatenate([high, high, low, zero], axis=1)


def split2(values):
    high = values.astype(bf16)
    low = (values - high.astype(f32)).astype(bf16)
    return high, low


def vmem():
    return pl.BlockSpec(memory_space=pltpu.VMEM)


def smem():
    return pl.BlockSpec(memory_space=pltpu.SMEM)


def for_nodes(numbers, columns_hbm, chunks, sems, pair_places, visit):
    def fetch(pair, slot):
        row = 25 * lax.shift_right_logical(pair, 2) + 5 * (pair & 3)
        return pltpu.make_async_copy(
            columns_hbm.at[pl.ds(row, 4)], chunks.at[slot], sems.at[slot]
        )

    for slot in range(SLOTS):
        fetch(jnp.int32(slot), slot).start()

    def some_pairs(index, carry):
        for slot in range(SLOTS):
            pair = SLOTS * index + slot
            fetch(pair, slot).wait()
            a, b = lax.shift_right_logical(pair, 2), pair & 3
            for c in range(4):
                places = pair_places(a, b, c)
                for ex in range(EXB):
                    for ey in range(EYL):
                        for ez in range(EZ):
                            node = chunks[slot, c, 0, 64 * ex + 16 * ey + ez]
                            visit(places, c, ex, ey, ez, node)

            @pl.when(index < 16 // SLOTS - 1)
            def _():
                fetch(pair + SLOTS, slot).start()

        return carry

    lax.fori_loop(0, 16 // SLOTS, some_pairs, 0)

    def far_line(ix, iy, c_count):
        ex = jnp.minimum(lax.shift_right_logical(ix, 2), EXB - 1)
        ey = jnp.minimum(lax.shift_right_logical(iy, 2), EYL - 1)
        a, b = ix - 4 * ex, iy - 4 * ey
        start = 3200 * a + 640 * b + 64 * ex + 16 * ey
        for c in range(5 - c_count, 5) if c_count == 1 else range(c_count):
            places = pair_places(a, b, c)
            for ez in range(EZ - 1 if c == 4 else 0, EZ):
                visit(places, c, ex, ey, ez, numbers[start + 128 * c + ez])

    def last_plane(iy, carry):
        far_line(jnp.int32(NXN - 1), iy, 4)
        return carry

    lax.fori_loop(0, NYN, last_plane, 0)

    def last_row(ix, carry):
        far_line(ix, jnp.int32(NYN - 1), 4)
        return carry

    lax.fori_loop(0, NXN - 1, last_row, 0)

    def top(ix, carry):
        for iy in range(NYN):
            far_line(ix, jnp.int32(iy), 1)
        return carry

    lax.fori_loop(0, NXN, top, 0)


def for_blocks(count, unroll, body):
    def group(index, carry):
        for part in range(unroll):
            body(index * unroll + part)
        return carry

    lax.fori_loop(0, count // unroll, group, 0)


def gather_kernel(
    columns_hbm,
    numbers_hbm,
    sources_hbm,
    displacement_hbm,
    velocity_hbm,
    mass_hbm,
    shear_hbm,
    lame_hbm,
    weight_hbm,
    pulses_hbm,
    frequency_hbm,
    force_out,
    motion_out,
    speed_out,
    inverse_out,
    shear_out,
    lame_out,
    mixing,
    rows,
    table,
    lines,
    numbers,
    sources,
    displacement,
    velocity,
    mass,
    shear,
    lame,
    weight,
    pulses,
    frequency,
    sems,
    chunks,
    chunk_sems,
):
    copies = [
        pltpu.make_async_copy(source, target, sems.at[position])
        for position, (source, target) in enumerate(
            (
                (frequency_hbm, frequency),
                (pulses_hbm, pulses),
                (sources_hbm, sources),
                (displacement_hbm, displacement),
                (velocity_hbm, velocity),
                (mass_hbm, mass),
                (numbers_hbm, numbers),
                (shear_hbm, shear),
                (lame_hbm, lame),
                (weight_hbm, weight),
            )
        )
    ]
    for copy in copies:
        copy.start()
    for copy in copies[0:2]:
        copy.wait()
    index = lax.broadcasted_iota(jnp.int32, (NFREQ, EVENTS), 0)
    mixing[...] = jnp.zeros((24, 3 * EVENTS), f32)
    for s in range(2):
        chosen = (frequency[s : s + 1, :] == index).astype(f32).astype(bf16)
        wavelet = jnp.dot(pulses[...], chosen, preferred_element_type=f32)
        for k in range(STEP_TOTAL):
            for q in range(3):
                row = 6 * k + 2 * q + s
                mixing[row : row + 1, EVENTS * q : EVENTS * (q + 1)] = wavelet[k : k + 1]
    for copy in copies[3:6]:
        copy.wait()
    for q in range(3):
        rows[24 + 2 * q : 26 + 2 * q, 0:NODES_DEV] = displacement[q]
        rows[32 + 2 * q : 34 + 2 * q, 0:NODES_DEV] = velocity[q]
    rows[38:39, 0:NODES_DEV] = mass[...].reshape(1, NODES_DEV)
    copies[2].wait()
    flat = sources[...].reshape(3 * EVENTS, NODES_DEV)
    rows[0:24, 0:NODES_DEV] = jnp.dot(
        mixing[...].astype(bf16), flat, preferred_element_type=f32
    )

    def transpose_block(block):
        start = pl.multiple_of(block * 128, 128)
        block_rows = rows[:, pl.ds(start, 128)]
        filler = jnp.zeros((128 - 3 * COMPS, 128), f32)
        table[pl.ds(start, 128), :] = jnp.concatenate(
            [block_rows, block_rows, block_rows, filler], axis=0
        ).T

    for_blocks(NODE_BLOCKS, 6, transpose_block)
    for copy in copies[6:]:
        copy.wait()

    def line_places(a, b, c):
        return (a * NYN + b) * LINE + c

    def gather_node(place, c, ex, ey, ez, node):
        del c
        at = place + ((4 * ex * NYN + 4 * ey) * LINE + 4 * ez)
        lines[pl.ds(at, 1), :] = table[pl.ds(node, 1), :]

    for_nodes(numbers, columns_hbm, chunks, chunk_sems, line_places, gather_node)

    lanes = lanes_of(128)

    def element_rows(pair):
        a = lax.shift_right_logical(pair * 13, 6)
        b = pair - 5 * a
        for group in ((0, 1, 2), (3, 4)):
            mixed = None
            for position, c in reversed(list(enumerate(group))):
                pieces = []
                for ex in range(EXB):
                    for ey in range(EYL):
                        line = (4 * ex + a) * NYN + 4 * ey + b
                        pieces.append(lines[pl.ds(line * LINE + c, EZ, stride=4), :])
                whole = jnp.concatenate(pieces, axis=0)
                if mixed is None:
                    mixed = whole
                else:
                    mixed = jnp.where(lanes < COMPS * (position + 1), whole, mixed)
            turned = mixed.T
            for position, c in enumerate(group):
                point = pair * 5 + c
                base = COMPS * position
                force_out[pl.ds(point, 24, stride=128), :] = turned[base : base + 24]
                motion_out[pl.ds(point, 6, stride=128), :] = turned[base + 24 : base + 30]
                speed_out[pl.ds(point, 6, stride=128), :] = turned[base + 32 : base + 38]
                inverse_out[pl.ds(point, 1), :] = 1.0 / turned[base + 38 : base + 39]

    for_blocks(25, 1, element_rows)
    for point in range(125, 128):
        force_out[pl.ds(point, 24, stride=128), :] = jnp.zeros((24, 128), f32)
        motion_out[pl.ds(point, 6, stride=128), :] = jnp.zeros((6, 128), f32)
        speed_out[pl.ds(point, 6, stride=128), :] = jnp.zeros((6, 128), f32)
    inverse_out[125:128, :] = jnp.zeros((3, 128), f32)
    shear_out[0:125, :] = shear[...] * weight[0:125, :]
    shear_out[125:128, :] = jnp.zeros((3, 128), f32)
    lame_out[0:125, :] = lame[...] * weight[0:125, :]
    lame_out[125:128, :] = jnp.zeros((3, 128), f32)


def lanes_of(count):
    return lax.broadcasted_iota(jnp.int32, (count, 128), 1)


def balance_of(motion, force, step, shear, lame, gradient, divergence, balance, integral):
    fields = jnp.concatenate([motion[128 * j : 128 * j + 128, :] for j in range(6)], axis=1)
    high, low = split2(fields)
    grads = jnp.dot(
        gradient[...], jnp.concatenate([high, low, high], axis=0), preferred_element_type=f32
    )

    def grad(d, q, s):
        j = 2 * q + s
        return grads[128 * d : 128 * d + 128, 128 * j : 128 * j + 128]

    mu = shear[...]
    lam = lame[...]
    stress = {}
    for s in range(2):
        pressure = lam * (grad(0, 0, s) + grad(1, 1, s) + grad(2, 2, s))
        for d in range(3):
            for q in range(d, 3):
                value = mu * (grad(d, q, s) + grad(q, d, s))
                if q == d:
                    value = value + pressure
                stress[d, q, s] = stress[q, d, s] = split2(value)
    highs, lows = (
        jnp.concatenate(
            [
                jnp.concatenate([stress[d, j // 2, j % 2][part] for j in range(6)], axis=1)
                for d in range(3)
            ],
            axis=0,
        )
        for part in range(2)
    )
    internal = jnp.dot(
        divergence[...], jnp.concatenate([highs, lows, highs], axis=0), preferred_element_type=f32
    )
    for j in range(6):
        balance[128 * j : 128 * j + 128, :] = internal[:, 128 * j : 128 * j + 128]

    def weighted(d, q):
        row = 128 * d + 125
        return jnp.concatenate(
            [grads[row : row + 1, 128 * j : 128 * j + 128] for j in (2 * q, 2 * q + 1)], axis=0
        )

    third = (weighted(0, 0) + weighted(1, 1) + weighted(2, 2)) / 3.0
    integral[0:2, :] = weighted(0, 0) - third
    integral[2:4, :] = weighted(1, 1) - third
    integral[4:6, :] = 0.5 * (weighted(0, 1) + weighted(1, 0))
    integral[6:8, :] = 0.5 * (weighted(0, 2) + weighted(2, 0))
    integral[8:10, :] = 0.5 * (weighted(1, 2) + weighted(2, 1))

    lane = lanes_of(25)
    keep = lane % 16
    for j in range(6):
        base = 128 * j
        first = balance[pl.ds(base, 25, stride=5), :]
        last = balance[pl.ds(base + 4, 25, stride=5), :]
        balance[pl.ds(base, 25, stride=5), :] = first + jnp.where(
            keep != 0, pltpu.roll(last, 1, 1), 0.0
        )
        balance[pl.ds(base + 4, 25, stride=5), :] = last + jnp.where(
            keep != 15, pltpu.roll(first, 127, 1), 0.0
        )
    side = lanes_of(5) % 64
    for j in range(6):
        for a in range(5):
            base = 128 * j + 25 * a
            first = balance[base : base + 5, :]
            last = balance[base + 20 : base + 25, :]
            balance[base : base + 5, :] = first + jnp.where(
                side >= 16, pltpu.roll(last, 16, 1), 0.0
            )
            balance[base + 20 : base + 25, :] = last + jnp.where(
                side < 48, pltpu.roll(first, 112, 1), 0.0
            )
    for j in range(6):
        base = 128 * j
        first = balance[base : base + 25, :]
        last = balance[base + 100 : base + 125, :]
        balance[base : base + 25, :] = first + jnp.where(
            lane >= 64, pltpu.roll(last, 64, 1), 0.0
        )
        balance[base + 100 : base + 125, :] = last + jnp.where(
            lane < 64, pltpu.roll(first, 64, 1), 0.0
        )
    balance[...] = force[768 * step : 768 * step + 768, :] - balance[...]


def pack_cycle(balance, side, even_out, odd_out):
    lane = lanes_of(25)
    even = (side[0] & 1) == 0
    for g in range(3):
        near, far = 128 * g, 128 * (g + 3)
        low = jnp.where(
            lane < 64, balance[near : near + 25, :], pltpu.roll(balance[far : far + 25, :], 64, 1)
        )
        up = jnp.where(
            lane < 64,
            pltpu.roll(balance[near + 100 : near + 125, :], 64, 1),
            balance[far + 100 : far + 125, :],
        )
        even_out[32 * g : 32 * g + 25, :] = jnp.where(even, up, low)
        odd_out[32 * g : 32 * g + 25, :] = jnp.where(even, low, up)


def add_cycle(balance, side, even_in, odd_in):
    lane = lanes_of(25)
    even = (side[0] & 1) == 0
    for g in range(3):
        near, far = 128 * g, 128 * (g + 3)
        first = even_in[32 * g : 32 * g + 25, :]
        second = odd_in[32 * g : 32 * g + 25, :]
        up = jnp.where(even, first, second)
        low = jnp.where(even, second, first)
        balance[near : near + 25, :] += jnp.where(lane < 64, low, 0.0)
        balance[far : far + 25, :] += jnp.where(lane < 64, pltpu.roll(low, 64, 1), 0.0)
        balance[near + 100 : near + 125, :] += jnp.where(lane >= 64, pltpu.roll(up, 64, 1), 0.0)
        balance[far + 100 : far + 125, :] += jnp.where(lane >= 64, up, 0.0)


def turn(values, slots):
    return values if slots % 8 == 0 else pltpu.roll(values, (16 * slots) % 128, 1)


def pack_lat(balance, side, even_out, odd_out):
    slot = lanes_of(5) // 16 % 4
    even = (side[0] & 1) == 0
    for g in range(2):
        for a in range(5):
            low = jnp.zeros((5, 128), f32)
            up = jnp.zeros((5, 128), f32)
            for t in range(4):
                j = 4 * g + t
                if j >= 6:
                    break
                base = 128 * j + 25 * a
                low = jnp.where(slot == t, turn(balance[base : base + 5, :], t), low)
                up = jnp.where(slot == t, turn(balance[base + 20 : base + 25, :], t - 3), up)
            at = 32 * g + 5 * a
            even_out[at : at + 5, :] = jnp.where(even, up, low)
            odd_out[at : at + 5, :] = jnp.where(even, low, up)


def add_lat(balance, side, even_in, odd_in):
    slot = lanes_of(5) // 16 % 4
    even = (side[0] & 1) == 0
    for g in range(2):
        for a in range(5):
            at = 32 * g + 5 * a
            first = even_in[at : at + 5, :]
            second = odd_in[at : at + 5, :]
            up = jnp.where(even, first, second)
            low = jnp.where(even, second, first)
            for t in range(4):
                j = 4 * g + t
                if j >= 6:
                    break
                base = 128 * j + 25 * a
                balance[base : base + 5, :] += jnp.where(slot == 0, turn(low, -t), 0.0)
                balance[base + 20 : base + 25, :] += jnp.where(slot == 3, turn(up, 3 - t), 0.0)


def first_kernel(
    blk, motion, force, shear, lame, gradient, divergence, balance, integral, even_out, odd_out
):
    balance_of(motion, force, 0, shear, lame, gradient, divergence, balance, integral)
    pack_cycle(balance, blk, even_out, odd_out)


def middle_kernel(blk, lat, old, even_in, odd_in, balance, even_out, odd_out):
    balance[...] = old[...]
    add_cycle(balance, blk, even_in, odd_in)
    pack_lat(balance, lat, even_out, odd_out)


def advance(lat, old, even_in, odd_in, inverse, motion_in, speed_in, motion, speed, balance):
    balance[...] = old[...]
    add_lat(balance, lat, even_in, odd_in)
    scale = inverse[...]
    for j in range(6):
        part = slice(128 * j, 128 * j + 128)
        now = speed_in[part, :] + balance[part, :] * scale
        speed[part, :] = now
        motion[part, :] = motion_in[part, :] + now


def make_step_kernel(step):
    def step_kernel(
        blk,
        lat,
        old,
        even_in,
        odd_in,
        inverse,
        motion_in,
        speed_in,
        force,
        shear,
        lame,
        gradient,
        divergence,
        balance,
        motion,
        speed,
        integral,
        even_out,
        odd_out,
    ):
        advance(lat, old, even_in, odd_in, inverse, motion_in, speed_in, motion, speed, balance)
        balance_of(motion, force, step, shear, lame, gradient, divergence, balance, integral)
        pack_cycle(balance, blk, even_out, odd_out)

    return step_kernel


def last_kernel(
    columns_hbm,
    numbers,
    lat,
    old,
    even_in,
    odd_in,
    inverse,
    motion_in,
    speed_in,
    motion_out,
    speed_out,
    balance,
    state,
    points,
    table,
    chunks,
    chunk_sems,
):
    advance(
        lat,
        old,
        even_in,
        odd_in,
        inverse,
        motion_in,
        speed_in,
        state.at[0:768, :],
        state.at[768:1536, :],
        balance,
    )

    def point_rows(group):
        values = jnp.concatenate(
            [state[pl.ds(group * 8 + part, 16, stride=128), :] for part in range(8)], axis=0
        )
        start = pl.multiple_of(group * 128, 128)
        points[pl.ds(start, 128), :] = values.T

    for_blocks(16, 4, point_rows)
    part_of = lanes_of(1) // 16

    def point_places(a, b, c):
        point = 25 * a + 5 * b + c
        return lax.shift_right_logical(point, 3) * 128, part_of == (point & 7)

    def scatter_node(places, c, ex, ey, ez, node):
        del c
        at = places[0] + (64 * ex + 16 * ey + ez)
        table[pl.ds(node, 1), :] = jnp.where(places[1], points[pl.ds(at, 1), :], 0.0)

    for_nodes(numbers, columns_hbm, chunks, chunk_sems, point_places, scatter_node)

    def turned(start):
        values = table[pl.ds(start, 128), :].T
        total = values[0:16]
        for part in range(1, 8):
            total = total + values[16 * part : 16 * part + 16]
        return total

    def transpose_block(block):
        start = pl.multiple_of(block * 128, 128)
        values = turned(start)
        for q in range(3):
            motion_out[q, :, pl.ds(start, 128)] = values[2 * q : 2 * q + 2]
            speed_out[q, :, pl.ds(start, 128)] = values[6 + 2 * q : 8 + 2 * q]

    for_blocks(NODE_BLOCKS - 1, 7, transpose_block)
    start = 128 * (NODE_BLOCKS - 1)
    rest = NODES_DEV - start
    values = turned(start)
    for q in range(3):
        motion_out[q, :, start:NODES_DEV] = values[2 * q : 2 * q + 2, 0:rest]
        speed_out[q, :, start:NODES_DEV] = values[6 + 2 * q : 8 + 2 * q, 0:rest]


def spectrum_kernel(wide, first, second, third, fourth, out):
    values = jnp.concatenate([part[...] for part in (first, second, third, fourth)], axis=0)
    high, low = split2(values)
    zero = jnp.zeros((8, 128), bf16)
    out[...] = jnp.dot(
        wide[...], jnp.concatenate([high, low, high, zero], axis=0), preferred_element_type=f32
    )


def kept(*extent):
    return pltpu.VMEM(extent, f32)


def hold(*arrays):
    return tuple(pltpu.with_memory_space_constraint(array, pltpu.VMEM) for array in arrays)


def exchange(axis, odd, even, odd_pairs, even_pairs):
    odd = lax.ppermute(odd, axis, odd_pairs)
    even = lax.ppermute(even, axis, even_pairs)
    return odd, even


def limit(mebibytes):
    return pltpu.CompilerParams(vmem_limit_bytes=mebibytes * 1024 * 1024)


def local(
    displacement,
    velocity,
    lumped_mass,
    shear_modulus,
    lame_modulus,
    adjoint_sources,
    node_numbers,
    event_frequency,
):
    gradient, divergence, weight = (jnp.asarray(table) for table in operator_tables())
    pulses, wide = frequency_tables()
    blk = lax.axis_index("blk").astype(jnp.int32).reshape(1)
    lat = lax.axis_index("lat").astype(jnp.int32).reshape(1)
    numbers = node_numbers.reshape(125 * 128)
    columns = node_numbers.reshape(125, 1, 128)
    blk_count = lax.axis_size("blk")
    lat_count = lax.axis_size("lat")
    cycle_even = [(i, i ^ 1) for i in range(blk_count)]
    cycle_odd = [(i, (((i + 1) ^ 1) - 1) % blk_count) for i in range(blk_count)]
    lat_even = [(i, i ^ 1) for i in range(lat_count)]
    lat_odd = [(i, ((i + 1) ^ 1) - 1) for i in range(1, lat_count - 1)]

    force, motion, speed, inverse, shear, lame = pl.pallas_call(
        gather_kernel,
        out_shape=(
            kept(24 * 128, 128),
            kept(768, 128),
            kept(768, 128),
            kept(128, 128),
            kept(128, 128),
            kept(128, 128),
        ),
        in_specs=[pl.BlockSpec(memory_space=pltpu.HBM)] * 11,
        out_specs=[vmem()] * 6,
        scratch_shapes=[
            pltpu.VMEM((24, 3 * EVENTS), f32),
            pltpu.VMEM((COMPS, NODE_BLOCKS * 128), f32),
            pltpu.VMEM((NODE_BLOCKS * 128, 128), f32),
            pltpu.VMEM((NXN * NYN * LINE, 128), f32),
            pltpu.SMEM((125 * 128,), jnp.int32),
            pltpu.VMEM((3, EVENTS, NODES_DEV), bf16),
            pltpu.VMEM((3, 2, NODES_DEV), f32),
            pltpu.VMEM((3, 2, NODES_DEV), f32),
            pltpu.VMEM((NODES_DEV,), f32),
            pltpu.VMEM((125, 128), f32),
            pltpu.VMEM((125, 128), f32),
            pltpu.VMEM((128, 128), f32),
            pltpu.VMEM((8, NFREQ), bf16),
            pltpu.VMEM((2, EVENTS), jnp.int32),
            pltpu.SemaphoreType.DMA((10,)),
            pltpu.SMEM((SLOTS, 4, 1, 128), jnp.int32),
            pltpu.SemaphoreType.DMA((SLOTS,)),
        ],
        compiler_params=limit(24),
        name="gather",
    )(
        *(
            pltpu.with_memory_space_constraint(array, pltpu.HBM)
            for array in (
                columns,
                numbers,
                adjoint_sources.transpose(1, 0, 2),
                displacement.transpose(1, 0, 2),
                velocity.transpose(1, 0, 2),
                lumped_mass,
                shear_modulus,
                lame_modulus,
                weight,
                jnp.asarray(pulses),
                event_frequency,
            )
        )
    )
    force, motion, speed, inverse, shear, lame, gradient, divergence = hold(
        force, motion, speed, inverse, shear, lame, gradient, divergence
    )
    balance_shape, integral_shape = kept(768, 128), kept(10, 128)
    cycle_shape, lat_shape = kept(96, 128), kept(64, 128)
    integrals = []
    for step in range(STEP_TOTAL):
        if step == 0:
            balance, integral, even, odd = pl.pallas_call(
                first_kernel,
                out_shape=(balance_shape, integral_shape, cycle_shape, cycle_shape),
                in_specs=[smem()] + [vmem()] * 6,
                out_specs=[vmem()] * 4,
                compiler_params=limit(8),
                name="first",
            )(blk, motion, force, shear, lame, gradient, divergence)
        else:
            balance, motion, speed, integral, even, odd = pl.pallas_call(
                make_step_kernel(step),
                out_shape=(
                    balance_shape,
                    balance_shape,
                    balance_shape,
                    integral_shape,
                    cycle_shape,
                    cycle_shape,
                ),
                in_specs=[smem()] * 2 + [vmem()] * 11,
                out_specs=[vmem()] * 6,
                compiler_params=limit(8),
                name="step",
            )(
                blk,
                lat,
                balance,
                even,
                odd,
                inverse,
                motion,
                speed,
                force,
                shear,
                lame,
                gradient,
                divergence,
            )
            motion, speed = hold(motion, speed)
        integrals.append(integral)
        odd, even = exchange("blk", odd, even, cycle_odd, cycle_even)
        balance, even, odd = pl.pallas_call(
            middle_kernel,
            out_shape=(balance_shape, lat_shape, lat_shape),
            in_specs=[smem()] * 2 + [vmem()] * 3,
            out_specs=[vmem()] * 3,
            compiler_params=limit(8),
            name="middle",
        )(blk, lat, *hold(balance, even, odd))
        odd, even = exchange("lat", odd, even, lat_odd, lat_even)
        balance, even, odd = hold(balance, even, odd)
    spectrum = pl.pallas_call(
        spectrum_kernel,
        out_shape=jax.ShapeDtypeStruct((640, 128), f32),
        in_specs=[vmem()] * 5,
        out_specs=vmem(),
        compiler_params=limit(8),
        name="spectrum",
    )(*hold(jnp.asarray(wide), *integrals))
    nodal = jax.ShapeDtypeStruct((3, 2, NODES_DEV), f32)
    final_motion, final_speed = pl.pallas_call(
        last_kernel,
        out_shape=(nodal, nodal),
        in_specs=[pl.BlockSpec(memory_space=pltpu.HBM)] + [smem()] * 2 + [vmem()] * 6,
        out_specs=[vmem()] * 2,
        scratch_shapes=[
            pltpu.VMEM((768, 128), f32),
            pltpu.VMEM((2048, 128), f32),
            pltpu.VMEM((16 * 128, 128), f32),
            pltpu.VMEM((NODE_BLOCKS * 128, 128), f32),
            pltpu.SMEM((SLOTS, 4, 1, 128), jnp.int32),
            pltpu.SemaphoreType.DMA((SLOTS,)),
        ],
        compiler_params=limit(24),
        name="last",
    )(
        pltpu.with_memory_space_constraint(columns, pltpu.HBM),
        numbers,
        lat,
        balance,
        even,
        odd,
        inverse,
        motion,
        speed,
    )
    return (
        final_motion.transpose(1, 0, 2),
        final_speed.transpose(1, 0, 2),
        spectrum.reshape(2, NFREQ, 5, 2, 128).transpose(0, 1, 3, 2, 4),
    )


def solution(mesh):
    nodes = P(None, None, ("blk", "lat"))
    columns = P(None, ("blk", "lat"))
    return jax.shard_map(
        local,
        mesh=mesh,
        in_specs=(nodes, nodes, P(("blk", "lat")), columns, columns, nodes, columns, P()),
        out_specs=(nodes, nodes, P(None, None, None, None, ("blk", "lat"))),
        check_vma=False,
    )
```

```python
import math

import jax
import jax.numpy as jnp
import numpy as np
from jax import lax
from jax.experimental import pallas as pl
from jax.experimental.pallas import tpu as pltpu
from jax.sharding import PartitionSpec as P


EXB = 2
EYL = 4
EZ = 16
NFREQ = 32
EVENTS = 32
STEP_TOTAL = 4
NXN = 9
NYN = 17
NODES_DEV = 9945
NODE_BLOCKS = 78
LINE = 72
COMPS = 40
SLOTS = 4


bf16 = jnp.bfloat16
f32 = jnp.float32


def gll_numpy():
    points = np.array([-1.0, -math.sqrt(3.0 / 7.0), 0.0, math.sqrt(3.0 / 7.0), 1.0])
    weights = np.array([0.1, 49.0 / 90.0, 32.0 / 45.0, 49.0 / 90.0, 0.1])
    products = np.ones(5)
    for target in range(5):
        for source in range(5):
            if source != target:
                products[target] *= points[target] - points[source]
    derivative = np.zeros((5, 5))
    for target in range(5):
        for source in range(5):
            if source != target:
                derivative[target, source] = (
                    products[target] / products[source] / (points[target] - points[source])
                )
        derivative[target, target] = -np.sum(derivative[target])
    cube = weights[:, None, None] * weights[None, :, None] * weights[None, None, :] / 8.0
    return derivative, cube.reshape(125)


def split_np(matrix):
    high = np.asarray(matrix, np.float32).astype(bf16)
    low = (matrix - high.astype(np.float64)).astype(np.float32).astype(bf16)
    return high, low


def operator_tables():
    derivative, cube = gll_numpy()
    eye = np.eye(5)
    parts = [
        2.0 * np.kron(np.kron(derivative, eye), eye),
        2.0 * np.kron(np.kron(eye, derivative), eye),
        2.0 * np.kron(np.kron(eye, eye), derivative),
    ]
    forward = np.zeros((3, 128, 128))
    backward = np.zeros((128, 3, 128))
    for d in range(3):
        forward[d, :125, :125] = parts[d]
        forward[d, 125, :125] = cube @ parts[d]
        backward[:125, d, :125] = parts[d].T
    fwd_high, fwd_low = split_np(forward.reshape(384, 128))
    bwd_high, bwd_low = split_np(backward.reshape(128, 384))
    gradient = np.concatenate([fwd_high, fwd_high, fwd_low], axis=1)
    divergence = np.concatenate([bwd_high, bwd_high, bwd_low], axis=1)
    weight = np.zeros((128, 128), np.float32)
    weight[:125] = cube[:, None]
    return gradient, divergence, weight


def frequency_tables():
    omega = np.pi * (1.0 + np.arange(NFREQ)) / (NFREQ + 1.0)
    times = 1.0 + np.arange(STEP_TOTAL)
    angles = omega[:, None] * times[None, :]
    pulses = np.zeros((8, NFREQ), np.float32)
    pulses[:STEP_TOTAL] = np.cos(angles).T
    pulses = pulses.astype(bf16)
    spectra = np.concatenate([np.cos(angles), -np.sin(angles)], axis=0)
    wide = np.einsum("rk,mn->rmkn", spectra, np.eye(10)).reshape(64 * 10, STEP_TOTAL * 10)
    high, low = split_np(wide)
    zero = np.zeros((640, 8), high.dtype)
    return pulses, np.concatenate([high, high, low, zero], axis=1)


def split2(values):
    high = values.astype(bf16)
    low = (values - high.astype(f32)).astype(bf16)
    return high, low


def vmem():
    return pl.BlockSpec(memory_space=pltpu.VMEM)


def hbm():
    return pl.BlockSpec(memory_space=pltpu.HBM)


def smem():
    return pl.BlockSpec(memory_space=pltpu.SMEM)


def start_pairs(numbers_hbm, chunks, sems, rounds, slots, pair_of):
    def fetch(index, slot):
        a, b = pair_of(index, slot)
        start = pl.multiple_of(128 * (25 * a + 5 * b), 128)
        return pltpu.make_async_copy(
            numbers_hbm.at[pl.ds(start, 512)], chunks.at[slot], sems.at[slot]
        )

    for slot in range(slots):
        fetch(jnp.int32(0), slot).start()

    def visit_pairs(pair_places, visit):
        def one_round(index, carry):
            for slot in range(slots):
                a, b = pair_of(index, slot)
                fetch(index, slot).wait()
                for c in range(4):
                    places = pair_places(a, b, c)
                    for ex in range(EXB):
                        for ey in range(EYL):
                            for ez in range(EZ):
                                node = chunks[slot, 128 * c + 64 * ex + 16 * ey + ez]
                                visit(places, c, ex, ey, ez, node)
                if rounds > 1:

                    @pl.when(index < rounds - 1)
                    def _():
                        fetch(index + 1, slot).start()

            return carry

        lax.fori_loop(0, rounds, one_round, 0)

    return visit_pairs


def visit_line(numbers, ix, iy, points, pair_places, visit):
    ex = jnp.minimum(lax.shift_right_logical(ix, 2), EXB - 1)
    ey = jnp.minimum(lax.shift_right_logical(iy, 2), EYL - 1)
    a, b = ix - 4 * ex, iy - 4 * ey
    start = 3200 * a + 640 * b + 64 * ex + 16 * ey
    for c in points:
        places = pair_places(a, b, c)
        for ez in range(EZ - 1 if c == 4 else 0, EZ):
            visit(places, c, ex, ey, ez, numbers[start + 128 * c + ez])


def visit_far(numbers, plane_rows, last_row, top_rows, pair_places, visit):
    first, count = plane_rows

    def plane_line(index, carry):
        visit_line(numbers, jnp.int32(NXN - 1), index + first, range(4), pair_places, visit)
        return carry

    lax.fori_loop(0, count, plane_line, 0)
    if last_row:

        def row_line(ix, carry):
            visit_line(numbers, ix, jnp.int32(NYN - 1), range(4), pair_places, visit)
            return carry

        lax.fori_loop(0, NXN, row_line, 0)

    def top(ix, carry):
        for iy in top_rows:
            visit_line(numbers, ix, jnp.int32(iy), (4,), pair_places, visit)
        return carry

    lax.fori_loop(0, NXN, top, 0)


def for_blocks(count, unroll, body):
    def group(index, carry):
        for part in range(unroll):
            body(index * unroll + part)
        return carry

    lax.fori_loop(0, count // unroll, group, 0)


def gather_kernel(
    numbers_hbm,
    sources_hbm,
    displacement_hbm,
    velocity_hbm,
    mass_hbm,
    shear_hbm,
    lame_hbm,
    weight_hbm,
    pulses_hbm,
    frequency_hbm,
    gradient_hbm,
    divergence_hbm,
    blk,
    force_out,
    motion_out,
    speed_out,
    inverse_out,
    shear_out,
    lame_out,
    gradient,
    divergence,
    balance,
    integral,
    even_out,
    odd_out,
    mixing,
    rows,
    table,
    lines,
    numbers,
    sources,
    displacement,
    velocity,
    mass,
    shear,
    lame,
    weight,
    pulses,
    frequency,
    sems,
    chunks,
    chunk_sems,
):
    copies = [
        pltpu.make_async_copy(source, target, sems.at[position])
        for position, (source, target) in enumerate(
            (
                (frequency_hbm, frequency),
                (pulses_hbm, pulses),
                (sources_hbm, sources),
                (displacement_hbm, displacement),
                (velocity_hbm, velocity),
                (mass_hbm, mass),
                (numbers_hbm, numbers),
                (shear_hbm, shear),
                (lame_hbm, lame),
                (weight_hbm, weight),
                (gradient_hbm, gradient),
                (divergence_hbm, divergence),
            )
        )
    ]
    for copy in copies:
        copy.start()
    visit_pairs = start_pairs(
        numbers_hbm, chunks, chunk_sems, 4, 4, lambda index, slot: (index, slot)
    )
    for copy in copies[0:2]:
        copy.wait()
    index = lax.broadcasted_iota(jnp.int32, (NFREQ, EVENTS), 0)
    mixing[...] = jnp.zeros((24, 3 * EVENTS), f32)
    for s in range(2):
        chosen = (frequency[s : s + 1, :] == index).astype(f32).astype(bf16)
        wavelet = jnp.dot(pulses[...], chosen, preferred_element_type=f32)
        for k in range(STEP_TOTAL):
            for q in range(3):
                row = 6 * k + 2 * q + s
                mixing[row : row + 1, EVENTS * q : EVENTS * (q + 1)] = wavelet[k : k + 1]
    for copy in copies[3:6]:
        copy.wait()
    for q in range(3):
        rows[24 + 2 * q : 26 + 2 * q, 0:NODES_DEV] = displacement[q]
        rows[32 + 2 * q : 34 + 2 * q, 0:NODES_DEV] = velocity[q]
    rows[38:39, 0:NODES_DEV] = mass[...].reshape(1, NODES_DEV)
    copies[2].wait()
    flat = sources[...].reshape(3 * EVENTS, NODES_DEV)
    rows[0:24, 0:NODES_DEV] = jnp.dot(
        mixing[...].astype(bf16), flat, preferred_element_type=f32
    )

    def transpose_block(block):
        start = pl.multiple_of(block * 128, 128)
        block_rows = rows[:, pl.ds(start, 128)]
        filler = jnp.zeros((128 - 3 * COMPS, 128), f32)
        table[pl.ds(start, 128), :] = jnp.concatenate(
            [block_rows, block_rows, block_rows, filler], axis=0
        ).T

    for_blocks(NODE_BLOCKS, 6, transpose_block)
    for copy in copies[6:]:
        copy.wait()

    def line_places(a, b, c):
        return (a * NYN + b) * LINE + c

    def gather_node(place, c, ex, ey, ez, node):
        del c
        at = place + ((4 * ex * NYN + 4 * ey) * LINE + 4 * ez)
        lines[pl.ds(at, 1), :] = table[pl.ds(node, 1), :]

    visit_pairs(line_places, gather_node)
    visit_far(numbers, (0, NYN - 1), True, range(NYN), line_places, gather_node)

    lanes = lanes_of(128)

    def element_rows(pair):
        a = lax.shift_right_logical(pair * 13, 6)
        b = pair - 5 * a
        for group in ((0, 1, 2), (3, 4)):
            mixed = None
            for position, c in reversed(list(enumerate(group))):
                pieces = []
                for ex in range(EXB):
                    for ey in range(EYL):
                        line = (4 * ex + a) * NYN + 4 * ey + b
                        pieces.append(lines[pl.ds(line * LINE + c, EZ, stride=4), :])
                whole = jnp.concatenate(pieces, axis=0)
                if mixed is None:
                    mixed = whole
                else:
                    mixed = jnp.where(lanes < COMPS * (position + 1), whole, mixed)
            turned = mixed.T
            for position, c in enumerate(group):
                point = pair * 5 + c
                base = COMPS * position
                force_out[pl.ds(point, 24, stride=128), :] = turned[base : base + 24]
                motion_out[pl.ds(point, 6, stride=128), :] = turned[base + 24 : base + 30]
                speed_out[pl.ds(point, 6, stride=128), :] = turned[base + 32 : base + 38]
                inverse_out[pl.ds(point, 1), :] = 1.0 / turned[base + 38 : base + 39]

    for_blocks(25, 1, element_rows)
    for point in range(125, 128):
        force_out[pl.ds(point, 24, stride=128), :] = jnp.zeros((24, 128), f32)
        motion_out[pl.ds(point, 6, stride=128), :] = jnp.zeros((6, 128), f32)
        speed_out[pl.ds(point, 6, stride=128), :] = jnp.zeros((6, 128), f32)
    inverse_out[125:128, :] = jnp.zeros((3, 128), f32)
    shear_out[0:125, :] = shear[...] * weight[0:125, :]
    shear_out[125:128, :] = jnp.zeros((3, 128), f32)
    lame_out[0:125, :] = lame[...] * weight[0:125, :]
    lame_out[125:128, :] = jnp.zeros((3, 128), f32)
    balance_of(motion_out, force_out, 0, shear_out, lame_out, gradient, divergence, balance, integral)
    pack_cycle(balance, blk, even_out, odd_out)


def lanes_of(count):
    return lax.broadcasted_iota(jnp.int32, (count, 128), 1)


def balance_of(motion, force, step, shear, lame, gradient, divergence, balance, integral):
    fields = jnp.concatenate([motion[128 * j : 128 * j + 128, :] for j in range(6)], axis=1)
    high, low = split2(fields)
    grads = jnp.dot(
        gradient[...], jnp.concatenate([high, low, high], axis=0), preferred_element_type=f32
    )

    def grad(d, q, s):
        j = 2 * q + s
        return grads[128 * d : 128 * d + 128, 128 * j : 128 * j + 128]

    mu = shear[...]
    lam = lame[...]
    stress = {}
    for s in range(2):
        pressure = lam * (grad(0, 0, s) + grad(1, 1, s) + grad(2, 2, s))
        for d in range(3):
            for q in range(d, 3):
                value = mu * (grad(d, q, s) + grad(q, d, s))
                if q == d:
                    value = value + pressure
                stress[d, q, s] = stress[q, d, s] = split2(value)
    highs, lows = (
        jnp.concatenate(
            [
                jnp.concatenate([stress[d, j // 2, j % 2][part] for j in range(6)], axis=1)
                for d in range(3)
            ],
            axis=0,
        )
        for part in range(2)
    )
    internal = jnp.dot(
        divergence[...], jnp.concatenate([highs, lows, highs], axis=0), preferred_element_type=f32
    )
    for j in range(6):
        balance[128 * j : 128 * j + 128, :] = internal[:, 128 * j : 128 * j + 128]

    def weighted(d, q):
        row = 128 * d + 125
        return jnp.concatenate(
            [grads[row : row + 1, 128 * j : 128 * j + 128] for j in (2 * q, 2 * q + 1)], axis=0
        )

    third = (weighted(0, 0) + weighted(1, 1) + weighted(2, 2)) / 3.0
    integral[0:2, :] = weighted(0, 0) - third
    integral[2:4, :] = weighted(1, 1) - third
    integral[4:6, :] = 0.5 * (weighted(0, 1) + weighted(1, 0))
    integral[6:8, :] = 0.5 * (weighted(0, 2) + weighted(2, 0))
    integral[8:10, :] = 0.5 * (weighted(1, 2) + weighted(2, 1))

    lane = lanes_of(25)
    keep = lane % 16
    for j in range(6):
        base = 128 * j
        first = balance[pl.ds(base, 25, stride=5), :]
        last = balance[pl.ds(base + 4, 25, stride=5), :]
        balance[pl.ds(base, 25, stride=5), :] = first + jnp.where(
            keep != 0, pltpu.roll(last, 1, 1), 0.0
        )
        balance[pl.ds(base + 4, 25, stride=5), :] = last + jnp.where(
            keep != 15, pltpu.roll(first, 127, 1), 0.0
        )
    side = lanes_of(5) % 64
    for j in range(6):
        for a in range(5):
            base = 128 * j + 25 * a
            first = balance[base : base + 5, :]
            last = balance[base + 20 : base + 25, :]
            balance[base : base + 5, :] = first + jnp.where(
                side >= 16, pltpu.roll(last, 16, 1), 0.0
            )
            balance[base + 20 : base + 25, :] = last + jnp.where(
                side < 48, pltpu.roll(first, 112, 1), 0.0
            )
    for j in range(6):
        base = 128 * j
        first = balance[base : base + 25, :]
        last = balance[base + 100 : base + 125, :]
        balance[base : base + 25, :] = first + jnp.where(
            lane >= 64, pltpu.roll(last, 64, 1), 0.0
        )
        balance[base + 100 : base + 125, :] = last + jnp.where(
            lane < 64, pltpu.roll(first, 64, 1), 0.0
        )
    balance[...] = force[768 * step : 768 * step + 768, :] - balance[...]


def pack_cycle(balance, side, even_out, odd_out):
    lane = lanes_of(25)
    even = (side[0] & 1) == 0
    for g in range(3):
        near, far = 128 * g, 128 * (g + 3)
        low = jnp.where(
            lane < 64, balance[near : near + 25, :], pltpu.roll(balance[far : far + 25, :], 64, 1)
        )
        up = jnp.where(
            lane < 64,
            pltpu.roll(balance[near + 100 : near + 125, :], 64, 1),
            balance[far + 100 : far + 125, :],
        )
        even_out[32 * g : 32 * g + 25, :] = jnp.where(even, up, low)
        odd_out[32 * g : 32 * g + 25, :] = jnp.where(even, low, up)


def add_cycle(balance, side, even_in, odd_in):
    lane = lanes_of(25)
    even = (side[0] & 1) == 0
    for g in range(3):
        near, far = 128 * g, 128 * (g + 3)
        first = even_in[32 * g : 32 * g + 25, :]
        second = odd_in[32 * g : 32 * g + 25, :]
        up = jnp.where(even, first, second)
        low = jnp.where(even, second, first)
        balance[near : near + 25, :] += jnp.where(lane < 64, low, 0.0)
        balance[far : far + 25, :] += jnp.where(lane < 64, pltpu.roll(low, 64, 1), 0.0)
        balance[near + 100 : near + 125, :] += jnp.where(lane >= 64, pltpu.roll(up, 64, 1), 0.0)
        balance[far + 100 : far + 125, :] += jnp.where(lane >= 64, up, 0.0)


def turn(values, slots):
    return values if slots % 8 == 0 else pltpu.roll(values, (16 * slots) % 128, 1)


def pack_lat(balance, side, even_out, odd_out):
    slot = lanes_of(5) // 16 % 4
    even = (side[0] & 1) == 0
    for g in range(2):
        for a in range(5):
            low = jnp.zeros((5, 128), f32)
            up = jnp.zeros((5, 128), f32)
            for t in range(4):
                j = 4 * g + t
                if j >= 6:
                    break
                base = 128 * j + 25 * a
                low = jnp.where(slot == t, turn(balance[base : base + 5, :], t), low)
                up = jnp.where(slot == t, turn(balance[base + 20 : base + 25, :], t - 3), up)
            at = 32 * g + 5 * a
            even_out[at : at + 5, :] = jnp.where(even, up, low)
            odd_out[at : at + 5, :] = jnp.where(even, low, up)


def add_lat(balance, side, even_in, odd_in):
    slot = lanes_of(5) // 16 % 4
    even = (side[0] & 1) == 0
    for g in range(2):
        for a in range(5):
            at = 32 * g + 5 * a
            first = even_in[at : at + 5, :]
            second = odd_in[at : at + 5, :]
            up = jnp.where(even, first, second)
            low = jnp.where(even, second, first)
            for t in range(4):
                j = 4 * g + t
                if j >= 6:
                    break
                base = 128 * j + 25 * a
                balance[base : base + 5, :] += jnp.where(slot == 0, turn(low, -t), 0.0)
                balance[base + 20 : base + 25, :] += jnp.where(slot == 3, turn(up, 3 - t), 0.0)


def middle_kernel(blk, lat, old, even_in, odd_in, balance, even_out, odd_out):
    balance[...] = old[...]
    add_cycle(balance, blk, even_in, odd_in)
    pack_lat(balance, lat, even_out, odd_out)


def advance(lat, old, even_in, odd_in, inverse, motion_in, speed_in, motion, speed, balance):
    balance[...] = old[...]
    add_lat(balance, lat, even_in, odd_in)
    scale = inverse[...]
    for j in range(6):
        part = slice(128 * j, 128 * j + 128)
        now = speed_in[part, :] + balance[part, :] * scale
        speed[part, :] = now
        motion[part, :] = motion_in[part, :] + now


def make_step_kernel(step):
    def step_kernel(
        blk,
        lat,
        old,
        even_in,
        odd_in,
        inverse,
        motion_in,
        speed_in,
        force,
        shear,
        lame,
        gradient,
        divergence,
        balance,
        motion,
        speed,
        integral,
        even_out,
        odd_out,
    ):
        advance(lat, old, even_in, odd_in, inverse, motion_in, speed_in, motion, speed, balance)
        balance_of(motion, force, step, shear, lame, gradient, divergence, balance, integral)
        pack_cycle(balance, blk, even_out, odd_out)

    return step_kernel


def scatter_to(table, state, points):
    def point_rows(group):
        values = jnp.concatenate(
            [state[pl.ds(group * 8 + part, 16, stride=128), :] for part in range(8)], axis=0
        )
        start = pl.multiple_of(group * 128, 128)
        points[pl.ds(start, 128), :] = values.T

    for_blocks(16, 4, point_rows)
    part_of = lanes_of(1) // 16

    def point_places(a, b, c):
        point = 25 * a + 5 * b + c
        return lax.shift_right_logical(point, 3) * 128, part_of == (point & 7)

    def scatter_node(places, c, ex, ey, ez, node):
        del c
        at = places[0] + (64 * ex + 16 * ey + ez)
        table[pl.ds(node, 1), :] = jnp.where(places[1], points[pl.ds(at, 1), :], 0.0)

    return point_places, scatter_node


def state_of(balance, inverse, motion_in, speed_in, state):
    scale = inverse[...]
    for j in range(6):
        part = slice(128 * j, 128 * j + 128)
        now = speed_in[part, :] + balance[part, :] * scale
        state[768 + 128 * j : 896 + 128 * j, :] = now
        state[part, :] = motion_in[part, :] + now


def inner_kernel(
    numbers_hbm, balance, inverse, motion_in, speed_in, table, state, points, chunks, sems
):
    visit_pairs = start_pairs(
        numbers_hbm, chunks, sems, 3, 3, lambda index, slot: (index + 1, slot + 1)
    )
    state_of(balance, inverse, motion_in, speed_in, state)
    visit_pairs(*scatter_to(table, state, points))


def outer_kernel(
    numbers_hbm,
    balance,
    inverse,
    motion_in,
    speed_in,
    table_in,
    table,
    state,
    points,
    chunks,
    sems,
    numbers,
    whole_sem,
):
    del table_in
    whole = pltpu.make_async_copy(numbers_hbm, numbers, whole_sem)
    whole.start()
    visit_pairs = start_pairs(
        numbers_hbm, chunks, sems, 1, 3, lambda index, slot: (index, slot + 1)
    )
    state_of(balance, inverse, motion_in, speed_in, state)
    places, visit = scatter_to(table, state, points)
    visit_pairs(places, visit)
    whole.wait()
    visit_far(numbers, (1, NYN - 2), False, range(1, NYN - 1), places, visit)


def last_kernel(
    numbers_hbm,
    lat,
    old,
    even_in,
    odd_in,
    inverse,
    motion_in,
    speed_in,
    table_in,
    motion_out,
    speed_out,
    table,
    balance,
    state,
    points,
    chunks,
    sems,
    numbers,
    whole_sem,
):
    del table_in
    whole = pltpu.make_async_copy(numbers_hbm, numbers, whole_sem)
    whole.start()
    visit_pairs = start_pairs(numbers_hbm, chunks, sems, 1, 4, lambda index, slot: (slot, index))
    balance[...] = old[...]
    add_lat(balance, lat, even_in, odd_in)
    state_of(balance, inverse, motion_in, speed_in, state)
    places, visit = scatter_to(table, state, points)
    visit_pairs(places, visit)
    whole.wait()
    visit_far(numbers, (0, 1), True, (0, NYN - 1), places, visit)

    def turned(start):
        values = table[pl.ds(start, 128), :].T
        total = values[0:16]
        for part in range(1, 8):
            total = total + values[16 * part : 16 * part + 16]
        return total

    def transpose_block(block):
        start = pl.multiple_of(block * 128, 128)
        values = turned(start)
        for q in range(3):
            motion_out[q, :, pl.ds(start, 128)] = values[2 * q : 2 * q + 2]
            speed_out[q, :, pl.ds(start, 128)] = values[6 + 2 * q : 8 + 2 * q]

    for_blocks(NODE_BLOCKS - 1, 7, transpose_block)
    start = 128 * (NODE_BLOCKS - 1)
    rest = NODES_DEV - start
    values = turned(start)
    for q in range(3):
        motion_out[q, :, start:NODES_DEV] = values[2 * q : 2 * q + 2, 0:rest]
        speed_out[q, :, start:NODES_DEV] = values[6 + 2 * q : 8 + 2 * q, 0:rest]


def spectrum_kernel(wide, first, second, third, fourth, out):
    values = jnp.concatenate([part[...] for part in (first, second, third, fourth)], axis=0)
    high, low = split2(values)
    zero = jnp.zeros((8, 128), bf16)
    out[...] = jnp.dot(
        wide[...], jnp.concatenate([high, low, high, zero], axis=0), preferred_element_type=f32
    )


def kept(*extent):
    return pltpu.VMEM(extent, f32)


def hold(*arrays):
    return tuple(pltpu.with_memory_space_constraint(array, pltpu.VMEM) for array in arrays)


def exchange(axis, odd, even, odd_pairs, even_pairs):
    odd = lax.ppermute(odd, axis, odd_pairs)
    even = lax.ppermute(even, axis, even_pairs)
    return odd, even


def limit(mebibytes):
    return pltpu.CompilerParams(vmem_limit_bytes=mebibytes * 1024 * 1024)


def local(
    displacement,
    velocity,
    lumped_mass,
    shear_modulus,
    lame_modulus,
    adjoint_sources,
    node_numbers,
    event_frequency,
):
    gradient, divergence, weight = (jnp.asarray(table) for table in operator_tables())
    pulses, wide = frequency_tables()
    blk = lax.axis_index("blk").astype(jnp.int32).reshape(1)
    lat = lax.axis_index("lat").astype(jnp.int32).reshape(1)
    numbers = node_numbers.reshape(125 * 128)
    blk_count = lax.axis_size("blk")
    lat_count = lax.axis_size("lat")
    cycle_even = [(i, i ^ 1) for i in range(blk_count)]
    cycle_odd = [(i, (((i + 1) ^ 1) - 1) % blk_count) for i in range(blk_count)]
    lat_even = [(i, i ^ 1) for i in range(lat_count)]
    lat_odd = [(i, ((i + 1) ^ 1) - 1) for i in range(1, lat_count - 1)]

    balance_shape, integral_shape = kept(768, 128), kept(10, 128)
    cycle_shape, lat_shape = kept(96, 128), kept(64, 128)
    (
        force,
        motion,
        speed,
        inverse,
        shear,
        lame,
        gradient,
        divergence,
        balance,
        integral,
        even,
        odd,
    ) = pl.pallas_call(
        gather_kernel,
        out_shape=(
            kept(24 * 128, 128),
            kept(768, 128),
            kept(768, 128),
            kept(128, 128),
            kept(128, 128),
            kept(128, 128),
            pltpu.VMEM((384, 384), bf16),
            pltpu.VMEM((128, 1152), bf16),
            balance_shape,
            integral_shape,
            cycle_shape,
            cycle_shape,
        ),
        in_specs=[hbm()] * 12 + [smem()],
        out_specs=[vmem()] * 12,
        scratch_shapes=[
            pltpu.VMEM((24, 3 * EVENTS), f32),
            pltpu.VMEM((COMPS, NODE_BLOCKS * 128), f32),
            pltpu.VMEM((NODE_BLOCKS * 128, 128), f32),
            pltpu.VMEM((NXN * NYN * LINE, 128), f32),
            pltpu.SMEM((125 * 128,), jnp.int32),
            pltpu.VMEM((3, EVENTS, NODES_DEV), bf16),
            pltpu.VMEM((3, 2, NODES_DEV), f32),
            pltpu.VMEM((3, 2, NODES_DEV), f32),
            pltpu.VMEM((NODES_DEV,), f32),
            pltpu.VMEM((125, 128), f32),
            pltpu.VMEM((125, 128), f32),
            pltpu.VMEM((128, 128), f32),
            pltpu.VMEM((8, NFREQ), bf16),
            pltpu.VMEM((2, EVENTS), jnp.int32),
            pltpu.SemaphoreType.DMA((12,)),
            pltpu.SMEM((SLOTS, 512), jnp.int32),
            pltpu.SemaphoreType.DMA((SLOTS,)),
        ],
        compiler_params=limit(24),
        name="gather",
    )(
        *(
            pltpu.with_memory_space_constraint(array, pltpu.HBM)
            for array in (
                numbers,
                adjoint_sources.transpose(1, 0, 2),
                displacement.transpose(1, 0, 2),
                velocity.transpose(1, 0, 2),
                lumped_mass,
                shear_modulus,
                lame_modulus,
                weight,
                jnp.asarray(pulses),
                event_frequency,
                gradient,
                divergence,
            )
        ),
        blk,
    )
    force, motion, speed, inverse, shear, lame, gradient, divergence = hold(
        force, motion, speed, inverse, shear, lame, gradient, divergence
    )
    integrals = []
    numbers_hbm = pltpu.with_memory_space_constraint(numbers, pltpu.HBM)
    table_shape = kept(NODE_BLOCKS * 128, 128)
    scatter_scratch = [
        pltpu.VMEM((2048, 128), f32),
        pltpu.VMEM((16 * 128, 128), f32),
        pltpu.SMEM((SLOTS, 512), jnp.int32),
        pltpu.SemaphoreType.DMA((SLOTS,)),
    ]
    whole_scratch = [pltpu.SMEM((125 * 128,), jnp.int32), pltpu.SemaphoreType.DMA]
    for step in range(STEP_TOTAL):
        if step > 0:
            balance, motion, speed, integral, even, odd = pl.pallas_call(
                make_step_kernel(step),
                out_shape=(
                    balance_shape,
                    balance_shape,
                    balance_shape,
                    integral_shape,
                    cycle_shape,
                    cycle_shape,
                ),
                in_specs=[smem()] * 2 + [vmem()] * 11,
                out_specs=[vmem()] * 6,
                compiler_params=limit(8),
                name="step",
            )(
                blk,
                lat,
                balance,
                even,
                odd,
                inverse,
                motion,
                speed,
                force,
                shear,
                lame,
                gradient,
                divergence,
            )
            motion, speed = hold(motion, speed)
        integrals.append(integral)
        odd, even = exchange("blk", odd, even, cycle_odd, cycle_even)
        if step == STEP_TOTAL - 1:
            table = pl.pallas_call(
                inner_kernel,
                out_shape=table_shape,
                in_specs=[hbm()] + [vmem()] * 4,
                out_specs=vmem(),
                scratch_shapes=scatter_scratch,
                compiler_params=limit(16),
                name="inner",
            )(numbers_hbm, *hold(balance, inverse, motion, speed))
        balance, even, odd = pl.pallas_call(
            middle_kernel,
            out_shape=(balance_shape, lat_shape, lat_shape),
            in_specs=[smem()] * 2 + [vmem()] * 3,
            out_specs=[vmem()] * 3,
            compiler_params=limit(8),
            name="middle",
        )(blk, lat, *hold(balance, even, odd))
        odd, even = exchange("lat", odd, even, lat_odd, lat_even)
        balance, even, odd = hold(balance, even, odd)
    table = pl.pallas_call(
        outer_kernel,
        out_shape=table_shape,
        in_specs=[hbm()] + [vmem()] * 5,
        out_specs=vmem(),
        scratch_shapes=scatter_scratch + whole_scratch,
        input_output_aliases={5: 0},
        compiler_params=limit(16),
        name="outer",
    )(numbers_hbm, *hold(balance, inverse, motion, speed, table))
    spectrum = pl.pallas_call(
        spectrum_kernel,
        out_shape=jax.ShapeDtypeStruct((640, 128), f32),
        in_specs=[vmem()] * 5,
        out_specs=vmem(),
        compiler_params=limit(8),
        name="spectrum",
    )(*hold(jnp.asarray(wide), *integrals))
    nodal = jax.ShapeDtypeStruct((3, 2, NODES_DEV), f32)
    final_motion, final_speed, _ = pl.pallas_call(
        last_kernel,
        out_shape=(nodal, nodal, table_shape),
        in_specs=[hbm(), smem()] + [vmem()] * 7,
        out_specs=[vmem()] * 3,
        scratch_shapes=[pltpu.VMEM((768, 128), f32)] + scatter_scratch + whole_scratch,
        input_output_aliases={8: 2},
        compiler_params=limit(16),
        name="last",
    )(
        numbers_hbm,
        lat,
        *hold(balance, even, odd, inverse, motion, speed, table),
    )
    return (
        final_motion.transpose(1, 0, 2),
        final_speed.transpose(1, 0, 2),
        spectrum.reshape(2, NFREQ, 5, 2, 128).transpose(0, 1, 3, 2, 4),
    )


def solution(mesh):
    nodes = P(None, None, ("blk", "lat"))
    columns = P(None, ("blk", "lat"))
    return jax.shard_map(
        local,
        mesh=mesh,
        in_specs=(nodes, nodes, P(("blk", "lat")), columns, columns, nodes, columns, P()),
        out_specs=(nodes, nodes, P(None, None, None, None, ("blk", "lat"))),
        check_vma=False,
    )
```

```python
import math

import jax
import jax.numpy as jnp
import numpy as np
from jax import lax
from jax.experimental import pallas as pl
from jax.experimental.pallas import tpu as pltpu
from jax.sharding import PartitionSpec as P


EXB = 2
EYL = 4
EZ = 16
NFREQ = 32
EVENTS = 32
STEP_TOTAL = 4
NXN = 9
NODES_DEV = 9945
NODE_BLOCKS = 78
LINE = 72
COMPS = 40
PARTS = 6
PART = 13 * 128
REST = NODES_DEV - (PARTS - 1) * PART


bf16 = jnp.bfloat16
f32 = jnp.float32


def gll_numpy():
    points = np.array([-1.0, -math.sqrt(3.0 / 7.0), 0.0, math.sqrt(3.0 / 7.0), 1.0])
    weights = np.array([0.1, 49.0 / 90.0, 32.0 / 45.0, 49.0 / 90.0, 0.1])
    products = np.ones(5)
    for target in range(5):
        for source in range(5):
            if source != target:
                products[target] *= points[target] - points[source]
    derivative = np.zeros((5, 5))
    for target in range(5):
        for source in range(5):
            if source != target:
                derivative[target, source] = (
                    products[target] / products[source] / (points[target] - points[source])
                )
        derivative[target, target] = -np.sum(derivative[target])
    cube = weights[:, None, None] * weights[None, :, None] * weights[None, None, :] / 8.0
    return derivative, cube.reshape(125)


def split_np(matrix):
    high = np.asarray(matrix, np.float32).astype(bf16)
    low = (matrix - high.astype(np.float64)).astype(np.float32).astype(bf16)
    return high, low


def operator_tables():
    derivative, cube = gll_numpy()
    eye = np.eye(5)
    parts = [
        2.0 * np.kron(np.kron(derivative, eye), eye),
        2.0 * np.kron(np.kron(eye, derivative), eye),
        2.0 * np.kron(np.kron(eye, eye), derivative),
    ]
    forward = np.zeros((3, 128, 128))
    backward = np.zeros((128, 3, 128))
    for d in range(3):
        forward[d, :125, :125] = parts[d]
        forward[d, 125, :125] = cube @ parts[d]
        backward[:125, d, :125] = parts[d].T
    fwd_high, fwd_low = split_np(forward.reshape(384, 128))
    bwd_high, bwd_low = split_np(backward.reshape(128, 384))
    gradient = np.concatenate([fwd_high, fwd_high, fwd_low], axis=1)
    divergence = np.concatenate([bwd_high, bwd_high, bwd_low], axis=1)
    weight = np.zeros((128, 128), np.float32)
    weight[:125] = cube[:, None]
    return gradient, divergence, weight


def frequency_tables():
    omega = np.pi * (1.0 + np.arange(NFREQ)) / (NFREQ + 1.0)
    times = 1.0 + np.arange(STEP_TOTAL)
    angles = omega[:, None] * times[None, :]
    pulses = np.zeros((8, NFREQ), np.float32)
    pulses[:STEP_TOTAL] = np.cos(angles).T
    pulses = pulses.astype(bf16)
    spectra = np.concatenate([np.cos(angles), -np.sin(angles)], axis=0)
    wide = np.einsum("rk,mn->rmkn", spectra, np.eye(10)).reshape(64 * 10, STEP_TOTAL * 10)
    high, low = split_np(wide)
    zero = np.zeros((640, 8), high.dtype)
    return pulses, np.concatenate([high, high, low, zero], axis=1)


def split2(values):
    high = values.astype(bf16)
    low = (values - high.astype(f32)).astype(bf16)
    return high, low


def vmem():
    return pl.BlockSpec(memory_space=pltpu.VMEM)


def hbm():
    return pl.BlockSpec(memory_space=pltpu.HBM)


def smem():
    return pl.BlockSpec(memory_space=pltpu.SMEM)


BOTH = (0, 1)
ALL_ROWS = (0, 1, 2, 3)


def start_pairs(numbers_hbm, chunks, sems, rounds, pairs):
    def fetch(index, slot):
        a, b = pairs[slot][0](index), pairs[slot][1]
        start = pl.multiple_of(128 * (25 * a + 5 * b), 128)
        return pltpu.make_async_copy(
            numbers_hbm.at[pl.ds(start, 640)], chunks.at[pl.ds(640 * slot, 640)], sems.at[slot]
        )

    for slot in range(len(pairs)):
        fetch(jnp.int32(0), slot).start()

    def visit_pairs(pair_places, visit, between=None):
        def one_round(index, carry):
            for slot, (a_of, b, columns, rows) in enumerate(pairs):
                a = a_of(index)
                fetch(index, slot).wait()
                for c in range(5):
                    if between is not None and c in (0, 2):
                        between(index, slot, c // 2)
                    places = pair_places(a, b, c)
                    for ex in columns:
                        for ey in rows:
                            for ez in range(EZ - 1 if c == 4 else 0, EZ):
                                node = chunks[640 * slot + 128 * c + 64 * ex + 16 * ey + ez]
                                visit(places, c, ex, ey, ez, node)
                if rounds > 1:

                    @pl.when(index < rounds - 1)
                    def _():
                        fetch(index + 1, slot).start()

            return carry

        if rounds > 1:
            lax.fori_loop(0, rounds, one_round, 0)
        else:
            one_round(jnp.int32(0), 0)

    return visit_pairs


def fixed(value):
    return lambda index: jnp.int32(value)


def off_first(b):
    return ALL_ROWS if b > 0 else ALL_ROWS[1:]


MAIN_PAIRS = tuple((lambda index: index, b, BOTH, ALL_ROWS) for b in range(4))
FAR_PAIRS = (
    tuple((fixed(4), b, (1,), ALL_ROWS) for b in range(4))
    + tuple((fixed(a), 4, BOTH, (3,)) for a in range(4))
    + ((fixed(4), 4, (1,), (3,)),)
)
INNER_PAIRS = tuple((lambda index: index + 1, b, BOTH, off_first(b)) for b in range(4))
OUTER_PAIRS = tuple((fixed(0), b, BOTH, off_first(b)) for b in range(4)) + tuple(
    (fixed(4), b, (1,), off_first(b)) for b in range(4)
)
LAST_PAIRS = (
    tuple((fixed(a), 0, BOTH, (0,)) for a in range(4))
    + ((fixed(4), 0, (1,), (0,)),)
    + FAR_PAIRS[4:]
)


def for_blocks(count, unroll, body):
    def group(index, carry):
        for part in range(unroll):
            body(index * unroll + part)
        return carry

    lax.fori_loop(0, count // unroll, group, 0)


def gather_kernel(
    numbers_hbm,
    sources_hbm,
    displacement_hbm,
    velocity_hbm,
    mass_hbm,
    shear_hbm,
    lame_hbm,
    weight_hbm,
    pulses_hbm,
    frequency_hbm,
    gradient_hbm,
    divergence_hbm,
    blk,
    force_out,
    motion_out,
    speed_out,
    inverse_out,
    shear_out,
    lame_out,
    gradient,
    divergence,
    balance,
    integral,
    even_out,
    odd_out,
    mixing,
    rows,
    table,
    lines_0,
    lines_1,
    lines_2,
    lines_3,
    sources,
    displacement,
    velocity,
    mass,
    shear,
    lame,
    weight,
    pulses,
    frequency,
    sems,
    chunks,
    chunk_sems,
    far_chunks,
    far_sems,
):
    lines = (lines_0, lines_1, lines_2, lines_3)
    copies = [
        pltpu.make_async_copy(source, target, sems.at[position])
        for position, (source, target) in enumerate(
            (
                (frequency_hbm, frequency),
                (pulses_hbm, pulses),
                (displacement_hbm, displacement),
                (velocity_hbm, velocity),
                (mass_hbm, mass),
                (sources_hbm, sources),
                (shear_hbm, shear),
                (lame_hbm, lame),
                (weight_hbm, weight),
                (gradient_hbm, gradient),
                (divergence_hbm, divergence),
            )
        )
    ]

    for copy in copies:
        copy.start()
    visit_far = start_pairs(numbers_hbm, far_chunks, far_sems, 1, FAR_PAIRS)
    visit_pairs = start_pairs(numbers_hbm, chunks, chunk_sems, 4, MAIN_PAIRS)
    for copy in copies[0:2]:
        copy.wait()
    index = lax.broadcasted_iota(jnp.int32, (NFREQ, EVENTS), 0)
    mixing[...] = jnp.zeros((24, 3 * EVENTS), f32)
    for s in range(2):
        chosen = (frequency[s : s + 1, :] == index).astype(f32).astype(bf16)
        wavelet = jnp.dot(pulses[...], chosen, preferred_element_type=f32)
        for k in range(STEP_TOTAL):
            for q in range(3):
                row = 6 * k + 2 * q + s
                mixing[row : row + 1, EVENTS * q : EVENTS * (q + 1)] = wavelet[k : k + 1]
    for copy in copies[2:5]:
        copy.wait()
    for q in range(3):
        rows[24 + 2 * q : 26 + 2 * q, 0:NODES_DEV] = displacement[q]
        rows[32 + 2 * q : 34 + 2 * q, 0:NODES_DEV] = velocity[q]
    rows[38:39, 0:NODES_DEV] = mass[...].reshape(1, NODES_DEV)
    mixed_events = mixing[...].astype(bf16)
    copies[5].wait()

    def force_rows(part):
        columns = pl.ds(pl.multiple_of(part * PART, 128), PART)
        flat = sources[:, :, columns].reshape(3 * EVENTS, PART)
        rows[0:24, columns] = jnp.dot(mixed_events, flat, preferred_element_type=f32)

    def node_rows(part):
        for block in range(PART // 128):
            start = pl.multiple_of(part * PART + block * 128, 128)
            block_rows = rows[:, pl.ds(start, 128)]
            filler = jnp.zeros((128 - 3 * COMPS, 128), f32)
            table[pl.ds(start, 128), :] = jnp.concatenate(
                [block_rows, block_rows, block_rows, filler], axis=0
            ).T

    force_rows(0)

    def one_part(part, carry):
        node_rows(part - 1)
        force_rows(part)
        return carry

    lax.fori_loop(1, PARTS - 1, one_part, 0)
    node_rows(PARTS - 2)
    flat = sources[:, :, NODES_DEV - REST :].reshape(3 * EVENTS, REST)
    rows[0:24, NODES_DEV - REST : NODES_DEV] = jnp.dot(
        mixed_events, flat, preferred_element_type=f32
    )
    node_rows(PARTS - 1)
    for copy in copies[6:]:
        copy.wait()

    def line_places(a, b, c):
        return lines[b % 4], (a * 5 + b // 4) * LINE + c

    def gather_node(places, c, ex, ey, ez, node):
        del c
        target, place = places
        at = place + ((20 * ex + ey) * LINE + 4 * ez)
        target[pl.ds(at, 1), :] = table[pl.ds(node, 1), :]

    lanes = lanes_of(128)

    def element_rows(a, b, part):
        group = ((0, 1, 2), (3, 4))[part]
        mixed = None
        for position, c in reversed(list(enumerate(group))):
            pieces = []
            for ex in range(EXB):
                for ey in range(EYL):
                    line = (4 * ex + a) * 5 + ey + b // 4
                    pieces.append(lines[b % 4][pl.ds(line * LINE + c, EZ, stride=4), :])
            whole = jnp.concatenate(pieces, axis=0)
            if mixed is None:
                mixed = whole
            else:
                mixed = jnp.where(lanes < COMPS * (position + 1), whole, mixed)
        turned = mixed.T
        for position, c in enumerate(group):
            point = 25 * a + 5 * b + c
            base = COMPS * position
            force_out[pl.ds(point, 24, stride=128), :] = turned[base : base + 24]
            motion_out[pl.ds(point, 6, stride=128), :] = turned[base + 24 : base + 30]
            speed_out[pl.ds(point, 6, stride=128), :] = turned[base + 32 : base + 38]
            inverse_out[pl.ds(point, 1), :] = 1.0 / turned[base + 38 : base + 39]

    def rows_before(index, slot, part):
        if slot == 0:
            element_rows(jnp.maximum(index - 1, 0), 3, part)
        else:
            element_rows(index, slot - 1, part)

    visit_far(line_places, gather_node)
    visit_pairs(line_places, gather_node, rows_before)

    def far_rows(a, carry):
        for part in range(2):
            element_rows(a, 4, part)
        return carry

    lax.fori_loop(0, 5, far_rows, 0)
    for a, b in ((3, 3), (4, 0), (4, 1), (4, 2), (4, 3)):
        for part in range(2):
            element_rows(a, b, part)
    for point in range(125, 128):
        force_out[pl.ds(point, 24, stride=128), :] = jnp.zeros((24, 128), f32)
        motion_out[pl.ds(point, 6, stride=128), :] = jnp.zeros((6, 128), f32)
        speed_out[pl.ds(point, 6, stride=128), :] = jnp.zeros((6, 128), f32)
    inverse_out[125:128, :] = jnp.zeros((3, 128), f32)
    shear_out[0:125, :] = shear[...] * weight[0:125, :]
    shear_out[125:128, :] = jnp.zeros((3, 128), f32)
    lame_out[0:125, :] = lame[...] * weight[0:125, :]
    lame_out[125:128, :] = jnp.zeros((3, 128), f32)
    balance_of(motion_out, force_out, 0, shear_out, lame_out, gradient, divergence, balance, integral)
    pack_cycle(balance, blk, even_out, odd_out)


def lanes_of(count):
    return lax.broadcasted_iota(jnp.int32, (count, 128), 1)


def balance_of(motion, force, step, shear, lame, gradient, divergence, balance, integral):
    fields = jnp.concatenate([motion[128 * j : 128 * j + 128, :] for j in range(6)], axis=1)
    high, low = split2(fields)
    grads = jnp.dot(
        gradient[...], jnp.concatenate([high, low, high], axis=0), preferred_element_type=f32
    )

    def grad(d, q, s):
        j = 2 * q + s
        return grads[128 * d : 128 * d + 128, 128 * j : 128 * j + 128]

    mu = shear[...]
    lam = lame[...]
    stress = {}
    for s in range(2):
        pressure = lam * (grad(0, 0, s) + grad(1, 1, s) + grad(2, 2, s))
        for d in range(3):
            for q in range(d, 3):
                value = mu * (grad(d, q, s) + grad(q, d, s))
                if q == d:
                    value = value + pressure
                stress[d, q, s] = stress[q, d, s] = split2(value)
    highs, lows = (
        jnp.concatenate(
            [
                jnp.concatenate([stress[d, j // 2, j % 2][part] for j in range(6)], axis=1)
                for d in range(3)
            ],
            axis=0,
        )
        for part in range(2)
    )
    internal = jnp.dot(
        divergence[...], jnp.concatenate([highs, lows, highs], axis=0), preferred_element_type=f32
    )
    for j in range(6):
        balance[128 * j : 128 * j + 128, :] = internal[:, 128 * j : 128 * j + 128]

    def weighted(d, q):
        row = 128 * d + 125
        return jnp.concatenate(
            [grads[row : row + 1, 128 * j : 128 * j + 128] for j in (2 * q, 2 * q + 1)], axis=0
        )

    third = (weighted(0, 0) + weighted(1, 1) + weighted(2, 2)) / 3.0
    integral[0:2, :] = weighted(0, 0) - third
    integral[2:4, :] = weighted(1, 1) - third
    integral[4:6, :] = 0.5 * (weighted(0, 1) + weighted(1, 0))
    integral[6:8, :] = 0.5 * (weighted(0, 2) + weighted(2, 0))
    integral[8:10, :] = 0.5 * (weighted(1, 2) + weighted(2, 1))

    lane = lanes_of(25)
    keep = lane % 16
    for j in range(6):
        base = 128 * j
        first = balance[pl.ds(base, 25, stride=5), :]
        last = balance[pl.ds(base + 4, 25, stride=5), :]
        balance[pl.ds(base, 25, stride=5), :] = first + jnp.where(
            keep != 0, pltpu.roll(last, 1, 1), 0.0
        )
        balance[pl.ds(base + 4, 25, stride=5), :] = last + jnp.where(
            keep != 15, pltpu.roll(first, 127, 1), 0.0
        )
    side = lanes_of(5) % 64
    for j in range(6):
        for a in range(5):
            base = 128 * j + 25 * a
            first = balance[base : base + 5, :]
            last = balance[base + 20 : base + 25, :]
            balance[base : base + 5, :] = first + jnp.where(
                side >= 16, pltpu.roll(last, 16, 1), 0.0
            )
            balance[base + 20 : base + 25, :] = last + jnp.where(
                side < 48, pltpu.roll(first, 112, 1), 0.0
            )
    for j in range(6):
        base = 128 * j
        first = balance[base : base + 25, :]
        last = balance[base + 100 : base + 125, :]
        balance[base : base + 25, :] = first + jnp.where(
            lane >= 64, pltpu.roll(last, 64, 1), 0.0
        )
        balance[base + 100 : base + 125, :] = last + jnp.where(
            lane < 64, pltpu.roll(first, 64, 1), 0.0
        )
    balance[...] = force[768 * step : 768 * step + 768, :] - balance[...]


def pack_cycle(balance, side, even_out, odd_out):
    lane = lanes_of(25)
    even = (side[0] & 1) == 0
    for g in range(3):
        near, far = 128 * g, 128 * (g + 3)
        low = jnp.where(
            lane < 64, balance[near : near + 25, :], pltpu.roll(balance[far : far + 25, :], 64, 1)
        )
        up = jnp.where(
            lane < 64,
            pltpu.roll(balance[near + 100 : near + 125, :], 64, 1),
            balance[far + 100 : far + 125, :],
        )
        even_out[32 * g : 32 * g + 25, :] = jnp.where(even, up, low)
        odd_out[32 * g : 32 * g + 25, :] = jnp.where(even, low, up)


def add_cycle(balance, side, even_in, odd_in):
    lane = lanes_of(25)
    even = (side[0] & 1) == 0
    for g in range(3):
        near, far = 128 * g, 128 * (g + 3)
        first = even_in[32 * g : 32 * g + 25, :]
        second = odd_in[32 * g : 32 * g + 25, :]
        up = jnp.where(even, first, second)
        low = jnp.where(even, second, first)
        balance[near : near + 25, :] += jnp.where(lane < 64, low, 0.0)
        balance[far : far + 25, :] += jnp.where(lane < 64, pltpu.roll(low, 64, 1), 0.0)
        balance[near + 100 : near + 125, :] += jnp.where(lane >= 64, pltpu.roll(up, 64, 1), 0.0)
        balance[far + 100 : far + 125, :] += jnp.where(lane >= 64, up, 0.0)


def turn(values, slots):
    return values if slots % 8 == 0 else pltpu.roll(values, (16 * slots) % 128, 1)


def pack_lat(balance, side, even_out, odd_out):
    slot = lanes_of(5) // 16 % 4
    even = (side[0] & 1) == 0
    for g in range(2):
        for a in range(5):
            low = jnp.zeros((5, 128), f32)
            up = jnp.zeros((5, 128), f32)
            for t in range(4):
                j = 4 * g + t
                if j >= 6:
                    break
                base = 128 * j + 25 * a
                low = jnp.where(slot == t, turn(balance[base : base + 5, :], t), low)
                up = jnp.where(slot == t, turn(balance[base + 20 : base + 25, :], t - 3), up)
            at = 32 * g + 5 * a
            even_out[at : at + 5, :] = jnp.where(even, up, low)
            odd_out[at : at + 5, :] = jnp.where(even, low, up)


def add_lat(balance, side, even_in, odd_in):
    slot = lanes_of(5) // 16 % 4
    even = (side[0] & 1) == 0
    for g in range(2):
        for a in range(5):
            at = 32 * g + 5 * a
            first = even_in[at : at + 5, :]
            second = odd_in[at : at + 5, :]
            up = jnp.where(even, first, second)
            low = jnp.where(even, second, first)
            for t in range(4):
                j = 4 * g + t
                if j >= 6:
                    break
                base = 128 * j + 25 * a
                balance[base : base + 5, :] += jnp.where(slot == 0, turn(low, -t), 0.0)
                balance[base + 20 : base + 25, :] += jnp.where(slot == 3, turn(up, 3 - t), 0.0)


def middle_kernel(blk, lat, old, even_in, odd_in, balance, even_out, odd_out):
    balance[...] = old[...]
    add_cycle(balance, blk, even_in, odd_in)
    pack_lat(balance, lat, even_out, odd_out)


def advance(lat, old, even_in, odd_in, inverse, motion_in, speed_in, motion, speed, balance):
    balance[...] = old[...]
    add_lat(balance, lat, even_in, odd_in)
    scale = inverse[...]
    for j in range(6):
        part = slice(128 * j, 128 * j + 128)
        now = speed_in[part, :] + balance[part, :] * scale
        speed[part, :] = now
        motion[part, :] = motion_in[part, :] + now


def make_step_kernel(step):
    def step_kernel(
        blk,
        lat,
        old,
        even_in,
        odd_in,
        inverse,
        motion_in,
        speed_in,
        force,
        shear,
        lame,
        gradient,
        divergence,
        balance,
        motion,
        speed,
        integral,
        even_out,
        odd_out,
    ):
        advance(lat, old, even_in, odd_in, inverse, motion_in, speed_in, motion, speed, balance)
        balance_of(motion, force, step, shear, lame, gradient, divergence, balance, integral)
        pack_cycle(balance, blk, even_out, odd_out)

    return step_kernel


def scatter_to(table, state, points):
    def point_rows(group):
        values = jnp.concatenate(
            [state[pl.ds(group * 8 + part, 16, stride=128), :] for part in range(8)], axis=0
        )
        start = pl.multiple_of(group * 128, 128)
        points[pl.ds(start, 128), :] = values.T

    for_blocks(16, 4, point_rows)
    part_of = lanes_of(1) // 16

    def point_places(a, b, c):
        point = 25 * a + 5 * b + c
        return lax.shift_right_logical(point, 3) * 128, part_of == (point & 7)

    def scatter_node(places, c, ex, ey, ez, node):
        del c
        at = places[0] + (64 * ex + 16 * ey + ez)
        table[pl.ds(node, 1), :] = jnp.where(places[1], points[pl.ds(at, 1), :], 0.0)

    return point_places, scatter_node


def state_of(balance, inverse, motion_in, speed_in, state):
    scale = inverse[...]
    for j in range(6):
        part = slice(128 * j, 128 * j + 128)
        now = speed_in[part, :] + balance[part, :] * scale
        state[768 + 128 * j : 896 + 128 * j, :] = now
        state[part, :] = motion_in[part, :] + now


def inner_kernel(
    numbers_hbm, balance, inverse, motion_in, speed_in, table, state, points, chunks, sems
):
    visit_pairs = start_pairs(numbers_hbm, chunks, sems, 3, INNER_PAIRS)
    state_of(balance, inverse, motion_in, speed_in, state)
    visit_pairs(*scatter_to(table, state, points))


def outer_kernel(
    numbers_hbm,
    balance,
    inverse,
    motion_in,
    speed_in,
    table_in,
    table,
    state,
    points,
    chunks,
    sems,
):
    del table_in
    visit_pairs = start_pairs(numbers_hbm, chunks, sems, 1, OUTER_PAIRS)
    state_of(balance, inverse, motion_in, speed_in, state)
    visit_pairs(*scatter_to(table, state, points))


def last_kernel(
    numbers_hbm,
    lat,
    old,
    even_in,
    odd_in,
    inverse,
    motion_in,
    speed_in,
    table_in,
    motion_out,
    speed_out,
    table,
    balance,
    state,
    points,
    chunks,
    sems,
):
    del table_in
    visit_pairs = start_pairs(numbers_hbm, chunks, sems, 1, LAST_PAIRS)
    balance[...] = old[...]
    add_lat(balance, lat, even_in, odd_in)
    state_of(balance, inverse, motion_in, speed_in, state)
    visit_pairs(*scatter_to(table, state, points))

    def turned(start):
        values = table[pl.ds(start, 128), :].T
        total = values[0:16]
        for part in range(1, 8):
            total = total + values[16 * part : 16 * part + 16]
        return total

    def transpose_block(block):
        start = pl.multiple_of(block * 128, 128)
        values = turned(start)
        for q in range(3):
            motion_out[q, :, pl.ds(start, 128)] = values[2 * q : 2 * q + 2]
            speed_out[q, :, pl.ds(start, 128)] = values[6 + 2 * q : 8 + 2 * q]

    for_blocks(NODE_BLOCKS - 1, 7, transpose_block)
    start = 128 * (NODE_BLOCKS - 1)
    rest = NODES_DEV - start
    values = turned(start)
    for q in range(3):
        motion_out[q, :, start:NODES_DEV] = values[2 * q : 2 * q + 2, 0:rest]
        speed_out[q, :, start:NODES_DEV] = values[6 + 2 * q : 8 + 2 * q, 0:rest]


def spectrum_kernel(wide, first, second, third, fourth, out):
    values = jnp.concatenate([part[...] for part in (first, second, third, fourth)], axis=0)
    high, low = split2(values)
    zero = jnp.zeros((8, 128), bf16)
    out[...] = jnp.dot(
        wide[...], jnp.concatenate([high, low, high, zero], axis=0), preferred_element_type=f32
    )


def kept(*extent):
    return pltpu.VMEM(extent, f32)


def hold(*arrays):
    return tuple(pltpu.with_memory_space_constraint(array, pltpu.VMEM) for array in arrays)


def exchange(axis, odd, even, odd_pairs, even_pairs):
    odd = lax.ppermute(odd, axis, odd_pairs)
    even = lax.ppermute(even, axis, even_pairs)
    return odd, even


def chunk_scratch(pairs):
    return [pltpu.SMEM((640 * len(pairs),), jnp.int32), pltpu.SemaphoreType.DMA((len(pairs),))]


def limit(mebibytes):
    return pltpu.CompilerParams(vmem_limit_bytes=mebibytes * 1024 * 1024)


def local(
    displacement,
    velocity,
    lumped_mass,
    shear_modulus,
    lame_modulus,
    adjoint_sources,
    node_numbers,
    event_frequency,
):
    gradient, divergence, weight = (jnp.asarray(table) for table in operator_tables())
    pulses, wide = frequency_tables()
    blk = lax.axis_index("blk").astype(jnp.int32).reshape(1)
    lat = lax.axis_index("lat").astype(jnp.int32).reshape(1)
    numbers = node_numbers.reshape(125 * 128)
    blk_count = lax.axis_size("blk")
    lat_count = lax.axis_size("lat")
    cycle_even = [(i, i ^ 1) for i in range(blk_count)]
    cycle_odd = [(i, (((i + 1) ^ 1) - 1) % blk_count) for i in range(blk_count)]
    lat_even = [(i, i ^ 1) for i in range(lat_count)]
    lat_odd = [(i, ((i + 1) ^ 1) - 1) for i in range(1, lat_count - 1)]

    balance_shape, integral_shape = kept(768, 128), kept(10, 128)
    cycle_shape, lat_shape = kept(96, 128), kept(64, 128)
    (
        force,
        motion,
        speed,
        inverse,
        shear,
        lame,
        gradient,
        divergence,
        balance,
        integral,
        even,
        odd,
    ) = pl.pallas_call(
        gather_kernel,
        out_shape=(
            kept(24 * 128, 128),
            kept(768, 128),
            kept(768, 128),
            kept(128, 128),
            kept(128, 128),
            kept(128, 128),
            pltpu.VMEM((384, 384), bf16),
            pltpu.VMEM((128, 1152), bf16),
            balance_shape,
            integral_shape,
            cycle_shape,
            cycle_shape,
        ),
        in_specs=[hbm()] * 12 + [smem()],
        out_specs=[vmem()] * 12,
        scratch_shapes=[
            pltpu.VMEM((24, 3 * EVENTS), f32),
            pltpu.VMEM((COMPS, NODE_BLOCKS * 128), f32),
            pltpu.VMEM((NODE_BLOCKS * 128, 128), f32),
            *[pltpu.VMEM((NXN * 5 * LINE, 128), f32)] * 4,
            pltpu.VMEM((3, EVENTS, NODES_DEV), bf16),
            pltpu.VMEM((3, 2, NODES_DEV), f32),
            pltpu.VMEM((3, 2, NODES_DEV), f32),
            pltpu.VMEM((NODES_DEV,), f32),
            pltpu.VMEM((125, 128), f32),
            pltpu.VMEM((125, 128), f32),
            pltpu.VMEM((128, 128), f32),
            pltpu.VMEM((8, NFREQ), bf16),
            pltpu.VMEM((2, EVENTS), jnp.int32),
            pltpu.SemaphoreType.DMA((11,)),
            *chunk_scratch(MAIN_PAIRS),
            *chunk_scratch(FAR_PAIRS),
        ],
        compiler_params=limit(24),
        name="gather",
    )(
        *(
            pltpu.with_memory_space_constraint(array, pltpu.HBM)
            for array in (
                numbers,
                adjoint_sources.transpose(1, 0, 2),
                displacement.transpose(1, 0, 2),
                velocity.transpose(1, 0, 2),
                lumped_mass,
                shear_modulus,
                lame_modulus,
                weight,
                jnp.asarray(pulses),
                event_frequency,
                gradient,
                divergence,
            )
        ),
        blk,
    )
    force, motion, speed, inverse, shear, lame, gradient, divergence = hold(
        force, motion, speed, inverse, shear, lame, gradient, divergence
    )
    integrals = []
    numbers_hbm = pltpu.with_memory_space_constraint(numbers, pltpu.HBM)
    table_shape = kept(NODE_BLOCKS * 128, 128)
    scatter_scratch = [pltpu.VMEM((2048, 128), f32), pltpu.VMEM((16 * 128, 128), f32)]
    for step in range(STEP_TOTAL):
        if step > 0:
            balance, motion, speed, integral, even, odd = pl.pallas_call(
                make_step_kernel(step),
                out_shape=(
                    balance_shape,
                    balance_shape,
                    balance_shape,
                    integral_shape,
                    cycle_shape,
                    cycle_shape,
                ),
                in_specs=[smem()] * 2 + [vmem()] * 11,
                out_specs=[vmem()] * 6,
                compiler_params=limit(8),
                name="step",
            )(
                blk,
                lat,
                balance,
                even,
                odd,
                inverse,
                motion,
                speed,
                force,
                shear,
                lame,
                gradient,
                divergence,
            )
            motion, speed = hold(motion, speed)
        integrals.append(integral)
        odd, even = exchange("blk", odd, even, cycle_odd, cycle_even)
        if step == STEP_TOTAL - 1:
            table = pl.pallas_call(
                inner_kernel,
                out_shape=table_shape,
                in_specs=[hbm()] + [vmem()] * 4,
                out_specs=vmem(),
                scratch_shapes=scatter_scratch + chunk_scratch(INNER_PAIRS),
                compiler_params=limit(16),
                name="inner",
            )(numbers_hbm, *hold(balance, inverse, motion, speed))
        balance, even, odd = pl.pallas_call(
            middle_kernel,
            out_shape=(balance_shape, lat_shape, lat_shape),
            in_specs=[smem()] * 2 + [vmem()] * 3,
            out_specs=[vmem()] * 3,
            compiler_params=limit(8),
            name="middle",
        )(blk, lat, *hold(balance, even, odd))
        odd, even = exchange("lat", odd, even, lat_odd, lat_even)
        balance, even, odd = hold(balance, even, odd)
    table = pl.pallas_call(
        outer_kernel,
        out_shape=table_shape,
        in_specs=[hbm()] + [vmem()] * 5,
        out_specs=vmem(),
        scratch_shapes=scatter_scratch + chunk_scratch(OUTER_PAIRS),
        input_output_aliases={5: 0},
        compiler_params=limit(16),
        name="outer",
    )(numbers_hbm, *hold(balance, inverse, motion, speed, table))
    spectrum = pl.pallas_call(
        spectrum_kernel,
        out_shape=jax.ShapeDtypeStruct((640, 128), f32),
        in_specs=[vmem()] * 5,
        out_specs=vmem(),
        compiler_params=limit(8),
        name="spectrum",
    )(*hold(jnp.asarray(wide), *integrals))
    nodal = jax.ShapeDtypeStruct((3, 2, NODES_DEV), f32)
    final_motion, final_speed, _ = pl.pallas_call(
        last_kernel,
        out_shape=(nodal, nodal, table_shape),
        in_specs=[hbm(), smem()] + [vmem()] * 7,
        out_specs=[vmem()] * 3,
        scratch_shapes=[pltpu.VMEM((768, 128), f32)] + scatter_scratch + chunk_scratch(LAST_PAIRS),
        input_output_aliases={8: 2},
        compiler_params=limit(16),
        name="last",
    )(
        numbers_hbm,
        lat,
        *hold(balance, even, odd, inverse, motion, speed, table),
    )
    return (
        final_motion.transpose(1, 0, 2),
        final_speed.transpose(1, 0, 2),
        spectrum.reshape(2, NFREQ, 5, 2, 128).transpose(0, 1, 3, 2, 4),
    )


def solution(mesh):
    nodes = P(None, None, ("blk", "lat"))
    columns = P(None, ("blk", "lat"))
    return jax.shard_map(
        local,
        mesh=mesh,
        in_specs=(nodes, nodes, P(("blk", "lat")), columns, columns, nodes, columns, P()),
        out_specs=(nodes, nodes, P(None, None, None, None, ("blk", "lat"))),
        check_vma=False,
    )
```

```python
import math

import jax
import jax.numpy as jnp
import numpy as np
from jax import lax
from jax.experimental import pallas as pl
from jax.experimental.pallas import tpu as pltpu
from jax.sharding import PartitionSpec as P


EXB = 2
EYL = 4
EZ = 16
NFREQ = 32
EVENTS = 32
STEP_TOTAL = 4
NXN = 9
NODES_DEV = 9945
NODE_BLOCKS = 78
LINE = 72
COMPS = 40
PARTS = 6
PART = 13 * 128
REST = NODES_DEV - (PARTS - 1) * PART


bf16 = jnp.bfloat16
f32 = jnp.float32


def gll_numpy():
    points = np.array([-1.0, -math.sqrt(3.0 / 7.0), 0.0, math.sqrt(3.0 / 7.0), 1.0])
    weights = np.array([0.1, 49.0 / 90.0, 32.0 / 45.0, 49.0 / 90.0, 0.1])
    products = np.ones(5)
    for target in range(5):
        for source in range(5):
            if source != target:
                products[target] *= points[target] - points[source]
    derivative = np.zeros((5, 5))
    for target in range(5):
        for source in range(5):
            if source != target:
                derivative[target, source] = (
                    products[target] / products[source] / (points[target] - points[source])
                )
        derivative[target, target] = -np.sum(derivative[target])
    cube = weights[:, None, None] * weights[None, :, None] * weights[None, None, :] / 8.0
    return derivative, cube.reshape(125)


def split_np(matrix):
    high = np.asarray(matrix, np.float32).astype(bf16)
    low = (matrix - high.astype(np.float64)).astype(np.float32).astype(bf16)
    return high, low


def operator_tables():
    derivative, cube = gll_numpy()
    eye = np.eye(5)
    parts = [
        2.0 * np.kron(np.kron(derivative, eye), eye),
        2.0 * np.kron(np.kron(eye, derivative), eye),
        2.0 * np.kron(np.kron(eye, eye), derivative),
    ]
    forward = np.zeros((3, 128, 128))
    backward = np.zeros((128, 3, 128))
    for d in range(3):
        forward[d, :125, :125] = parts[d]
        forward[d, 125, :125] = cube @ parts[d]
        backward[:125, d, :125] = parts[d].T
    fwd_high, fwd_low = split_np(forward.reshape(384, 128))
    bwd_high, bwd_low = split_np(backward.reshape(128, 384))
    gradient = np.concatenate([fwd_high, fwd_high, fwd_low], axis=1)
    divergence = np.concatenate([bwd_high, bwd_high, bwd_low], axis=1)
    weight = np.zeros((128, 128), np.float32)
    weight[:125] = cube[:, None]
    return gradient, divergence, weight


def frequency_tables():
    omega = np.pi * (1.0 + np.arange(NFREQ)) / (NFREQ + 1.0)
    times = 1.0 + np.arange(STEP_TOTAL)
    angles = omega[:, None] * times[None, :]
    pulses = np.zeros((8, NFREQ), np.float32)
    pulses[:STEP_TOTAL] = np.cos(angles).T
    pulses = pulses.astype(bf16)
    spectra = np.concatenate([np.cos(angles), -np.sin(angles)], axis=0)
    wide = np.einsum("rk,mn->rmkn", spectra, np.eye(10)).reshape(64 * 10, STEP_TOTAL * 10)
    high, low = split_np(wide)
    zero = np.zeros((640, 8), high.dtype)
    return pulses, np.concatenate([high, high, low, zero], axis=1)


def split2(values):
    high = values.astype(bf16)
    low = (values - high.astype(f32)).astype(bf16)
    return high, low


def vmem():
    return pl.BlockSpec(memory_space=pltpu.VMEM)


def hbm():
    return pl.BlockSpec(memory_space=pltpu.HBM)


def smem():
    return pl.BlockSpec(memory_space=pltpu.SMEM)


BOTH = (0, 1)
ALL_ROWS = (0, 1, 2, 3)


def start_pairs(numbers_hbm, chunks, sems, rounds, pairs):
    def fetch(index, slot):
        a, b = pairs[slot][0](index), pairs[slot][1]
        start = pl.multiple_of(128 * (25 * a + 5 * b), 128)
        return pltpu.make_async_copy(
            numbers_hbm.at[pl.ds(start, 640)], chunks.at[pl.ds(640 * slot, 640)], sems.at[slot]
        )

    for slot in range(len(pairs)):
        fetch(jnp.int32(0), slot).start()

    def visit_pairs(pair_places, visit, between=None):
        def one_round(index, carry):
            for slot, (a_of, b, columns, rows) in enumerate(pairs):
                a = a_of(index)
                fetch(index, slot).wait()
                for c in range(5):
                    if between is not None and c in (0, 2):
                        between(index, slot, c // 2)
                    places = pair_places(a, b, c)
                    for ex in columns:
                        for ey in rows:
                            for ez in range(EZ - 1 if c == 4 else 0, EZ):
                                node = chunks[640 * slot + 128 * c + 64 * ex + 16 * ey + ez]
                                visit(places, c, ex, ey, ez, node)
                if rounds > 1:

                    @pl.when(index < rounds - 1)
                    def _():
                        fetch(index + 1, slot).start()

            return carry

        if rounds > 1:
            lax.fori_loop(0, rounds, one_round, 0)
        else:
            one_round(jnp.int32(0), 0)

    return visit_pairs


def fixed(value):
    return lambda index: jnp.int32(value)


def off_first(b):
    return ALL_ROWS if b > 0 else ALL_ROWS[1:]


MAIN_PAIRS = tuple((lambda index: index, b, BOTH, ALL_ROWS) for b in range(4))
FAR_PAIRS = (
    tuple((fixed(4), b, (1,), ALL_ROWS) for b in range(4))
    + tuple((fixed(a), 4, BOTH, (3,)) for a in range(4))
    + ((fixed(4), 4, (1,), (3,)),)
)
INNER_PAIRS = tuple((lambda index: index + 1, b, BOTH, off_first(b)) for b in range(4))
OUTER_PAIRS = tuple((fixed(0), b, BOTH, off_first(b)) for b in range(4)) + tuple(
    (fixed(4), b, (1,), off_first(b)) for b in range(4)
)
LAST_PAIRS = (
    tuple((fixed(a), 0, BOTH, (0,)) for a in range(4))
    + ((fixed(4), 0, (1,), (0,)),)
    + FAR_PAIRS[4:]
)


def groups_of(planes, rows):
    return sorted({(25 * a + 5 * b + c) // 8 for a in planes for b in rows for c in range(5)})


INNER_GROUPS = groups_of((1, 2, 3), (0, 1, 2, 3))
OUTER_GROUPS = groups_of((0, 4), (0, 1, 2, 3))
LAST_GROUPS = groups_of((0, 1, 2, 3, 4), (0, 4))


def for_blocks(count, unroll, body):
    def group(index, carry):
        for part in range(unroll):
            body(index * unroll + part)
        return carry

    lax.fori_loop(0, count // unroll, group, 0)


def gather_kernel(
    numbers_hbm,
    sources_hbm,
    displacement_hbm,
    velocity_hbm,
    mass_hbm,
    shear_hbm,
    lame_hbm,
    weight_hbm,
    pulses_hbm,
    frequency_hbm,
    gradient_hbm,
    divergence_hbm,
    blk,
    force_out,
    motion_out,
    speed_out,
    inverse_out,
    shear_out,
    lame_out,
    gradient,
    divergence,
    balance,
    integral,
    faces,
    mixing,
    rows,
    table,
    lines_0,
    lines_1,
    lines_2,
    lines_3,
    sources,
    displacement,
    velocity,
    mass,
    shear,
    lame,
    weight,
    pulses,
    frequency,
    sems,
    chunks,
    chunk_sems,
    far_chunks,
    far_sems,
):
    lines = (lines_0, lines_1, lines_2, lines_3)
    copies = [
        pltpu.make_async_copy(source, target, sems.at[position])
        for position, (source, target) in enumerate(
            (
                (frequency_hbm, frequency),
                (pulses_hbm, pulses),
                (displacement_hbm, displacement),
                (velocity_hbm, velocity),
                (mass_hbm, mass),
                (sources_hbm, sources),
                (shear_hbm, shear),
                (lame_hbm, lame),
                (weight_hbm, weight),
                (gradient_hbm, gradient),
                (divergence_hbm, divergence),
            )
        )
    ]

    for copy in copies:
        copy.start()
    visit_far = start_pairs(numbers_hbm, far_chunks, far_sems, 1, FAR_PAIRS)
    visit_pairs = start_pairs(numbers_hbm, chunks, chunk_sems, 4, MAIN_PAIRS)
    for copy in copies[0:2]:
        copy.wait()
    index = lax.broadcasted_iota(jnp.int32, (NFREQ, EVENTS), 0)
    mixing[...] = jnp.zeros((24, 3 * EVENTS), f32)
    for s in range(2):
        chosen = (frequency[s : s + 1, :] == index).astype(f32).astype(bf16)
        wavelet = jnp.dot(pulses[...], chosen, preferred_element_type=f32)
        for k in range(STEP_TOTAL):
            for q in range(3):
                row = 6 * k + 2 * q + s
                mixing[row : row + 1, EVENTS * q : EVENTS * (q + 1)] = wavelet[k : k + 1]
    for copy in copies[2:5]:
        copy.wait()
    for q in range(3):
        rows[24 + 2 * q : 26 + 2 * q, 0:NODES_DEV] = displacement[q]
        rows[32 + 2 * q : 34 + 2 * q, 0:NODES_DEV] = velocity[q]
    rows[38:39, 0:NODES_DEV] = mass[...].reshape(1, NODES_DEV)
    mixed_events = mixing[...].astype(bf16)
    copies[5].wait()

    def force_rows(part):
        columns = pl.ds(pl.multiple_of(part * PART, 128), PART)
        flat = sources[:, :, columns].reshape(3 * EVENTS, PART)
        rows[0:24, columns] = jnp.dot(mixed_events, flat, preferred_element_type=f32)

    def node_rows(part):
        for block in range(PART // 128):
            start = pl.multiple_of(part * PART + block * 128, 128)
            block_rows = rows[:, pl.ds(start, 128)]
            filler = jnp.zeros((128 - 3 * COMPS, 128), f32)
            table[pl.ds(start, 128), :] = jnp.concatenate(
                [block_rows, block_rows, block_rows, filler], axis=0
            ).T

    force_rows(0)

    def one_part(part, carry):
        node_rows(part - 1)
        force_rows(part)
        return carry

    lax.fori_loop(1, PARTS - 1, one_part, 0)
    node_rows(PARTS - 2)
    flat = sources[:, :, NODES_DEV - REST :].reshape(3 * EVENTS, REST)
    rows[0:24, NODES_DEV - REST : NODES_DEV] = jnp.dot(
        mixed_events, flat, preferred_element_type=f32
    )
    node_rows(PARTS - 1)
    for copy in copies[6:]:
        copy.wait()

    def line_places(a, b, c):
        return lines[b % 4], (a * 5 + b // 4) * LINE + c

    def gather_node(places, c, ex, ey, ez, node):
        del c
        target, place = places
        at = place + ((20 * ex + ey) * LINE + 4 * ez)
        target[pl.ds(at, 1), :] = table[pl.ds(node, 1), :]

    lanes = lanes_of(128)

    def element_rows(a, b, part):
        group = ((0, 1, 2), (3, 4))[part]
        mixed = None
        for position, c in reversed(list(enumerate(group))):
            pieces = []
            for ex in range(EXB):
                for ey in range(EYL):
                    line = (4 * ex + a) * 5 + ey + b // 4
                    pieces.append(lines[b % 4][pl.ds(line * LINE + c, EZ, stride=4), :])
            whole = jnp.concatenate(pieces, axis=0)
            if mixed is None:
                mixed = whole
            else:
                mixed = jnp.where(lanes < COMPS * (position + 1), whole, mixed)
        turned = mixed.T
        for position, c in enumerate(group):
            point = 25 * a + 5 * b + c
            base = COMPS * position
            force_out[pl.ds(point, 24, stride=128), :] = turned[base : base + 24]
            motion_out[pl.ds(point, 6, stride=128), :] = turned[base + 24 : base + 30]
            speed_out[pl.ds(point, 6, stride=128), :] = turned[base + 32 : base + 38]
            inverse_out[pl.ds(point, 1), :] = 1.0 / turned[base + 38 : base + 39]

    def rows_before(index, slot, part):
        if slot == 0:
            element_rows(jnp.maximum(index - 1, 0), 3, part)
        else:
            element_rows(index, slot - 1, part)
        if slot == 3:
            element_rows(index, 4, part)

    visit_far(line_places, gather_node)
    visit_pairs(line_places, gather_node, rows_before)

    for a, b in ((3, 3), (4, 0), (4, 1), (4, 2), (4, 3), (4, 4)):
        for part in range(2):
            element_rows(a, b, part)
    for point in range(125, 128):
        force_out[pl.ds(point, 24, stride=128), :] = jnp.zeros((24, 128), f32)
        motion_out[pl.ds(point, 6, stride=128), :] = jnp.zeros((6, 128), f32)
        speed_out[pl.ds(point, 6, stride=128), :] = jnp.zeros((6, 128), f32)
    inverse_out[125:128, :] = jnp.zeros((3, 128), f32)
    shear_out[0:125, :] = shear[...] * weight[0:125, :]
    shear_out[125:128, :] = jnp.zeros((3, 128), f32)
    lame_out[0:125, :] = lame[...] * weight[0:125, :]
    lame_out[125:128, :] = jnp.zeros((3, 128), f32)
    balance_of(motion_out, force_out, 0, shear_out, lame_out, gradient, divergence, balance, integral)
    pack_cycle(balance, blk, faces.at[0:96, :], faces.at[96:192, :])


def lanes_of(count):
    return lax.broadcasted_iota(jnp.int32, (count, 128), 1)


def balance_of(motion, force, step, shear, lame, gradient, divergence, balance, integral):
    fields = jnp.concatenate([motion[128 * j : 128 * j + 128, :] for j in range(6)], axis=1)
    high, low = split2(fields)
    grads = jnp.dot(
        gradient[...], jnp.concatenate([high, low, high], axis=0), preferred_element_type=f32
    )

    def grad(d, q, s):
        j = 2 * q + s
        return grads[128 * d : 128 * d + 128, 128 * j : 128 * j + 128]

    mu = shear[...]
    lam = lame[...]
    stress = {}
    for s in range(2):
        pressure = lam * (grad(0, 0, s) + grad(1, 1, s) + grad(2, 2, s))
        for d in range(3):
            for q in range(d, 3):
                value = mu * (grad(d, q, s) + grad(q, d, s))
                if q == d:
                    value = value + pressure
                stress[d, q, s] = stress[q, d, s] = split2(value)
    highs, lows = (
        jnp.concatenate(
            [
                jnp.concatenate([stress[d, j // 2, j % 2][part] for j in range(6)], axis=1)
                for d in range(3)
            ],
            axis=0,
        )
        for part in range(2)
    )
    internal = jnp.dot(
        divergence[...], jnp.concatenate([highs, lows, highs], axis=0), preferred_element_type=f32
    )
    for j in range(6):
        balance[128 * j : 128 * j + 128, :] = internal[:, 128 * j : 128 * j + 128]

    def weighted(d, q):
        row = 128 * d + 125
        return jnp.concatenate(
            [grads[row : row + 1, 128 * j : 128 * j + 128] for j in (2 * q, 2 * q + 1)], axis=0
        )

    third = (weighted(0, 0) + weighted(1, 1) + weighted(2, 2)) / 3.0
    integral[0:2, :] = weighted(0, 0) - third
    integral[2:4, :] = weighted(1, 1) - third
    integral[4:6, :] = 0.5 * (weighted(0, 1) + weighted(1, 0))
    integral[6:8, :] = 0.5 * (weighted(0, 2) + weighted(2, 0))
    integral[8:10, :] = 0.5 * (weighted(1, 2) + weighted(2, 1))

    lane = lanes_of(25)
    keep = lane % 16
    for j in range(6):
        base = 128 * j
        first = balance[pl.ds(base, 25, stride=5), :]
        last = balance[pl.ds(base + 4, 25, stride=5), :]
        balance[pl.ds(base, 25, stride=5), :] = first + jnp.where(
            keep != 0, pltpu.roll(last, 1, 1), 0.0
        )
        balance[pl.ds(base + 4, 25, stride=5), :] = last + jnp.where(
            keep != 15, pltpu.roll(first, 127, 1), 0.0
        )
    side = lanes_of(5) % 64
    for j in range(6):
        for a in range(5):
            base = 128 * j + 25 * a
            first = balance[base : base + 5, :]
            last = balance[base + 20 : base + 25, :]
            balance[base : base + 5, :] = first + jnp.where(
                side >= 16, pltpu.roll(last, 16, 1), 0.0
            )
            balance[base + 20 : base + 25, :] = last + jnp.where(
                side < 48, pltpu.roll(first, 112, 1), 0.0
            )
    for j in range(6):
        base = 128 * j
        first = balance[base : base + 25, :]
        last = balance[base + 100 : base + 125, :]
        balance[base : base + 25, :] = first + jnp.where(
            lane >= 64, pltpu.roll(last, 64, 1), 0.0
        )
        balance[base + 100 : base + 125, :] = last + jnp.where(
            lane < 64, pltpu.roll(first, 64, 1), 0.0
        )
    balance[...] = force[768 * step : 768 * step + 768, :] - balance[...]


def pack_cycle(balance, side, even_out, odd_out):
    lane = lanes_of(25)
    even = (side[0] & 1) == 0
    for g in range(3):
        near, far = 128 * g, 128 * (g + 3)
        low = jnp.where(
            lane < 64, balance[near : near + 25, :], pltpu.roll(balance[far : far + 25, :], 64, 1)
        )
        up = jnp.where(
            lane < 64,
            pltpu.roll(balance[near + 100 : near + 125, :], 64, 1),
            balance[far + 100 : far + 125, :],
        )
        even_out[32 * g : 32 * g + 25, :] = jnp.where(even, up, low)
        odd_out[32 * g : 32 * g + 25, :] = jnp.where(even, low, up)


def add_cycle(balance, side, even_in, odd_in):
    lane = lanes_of(25)
    even = (side[0] & 1) == 0
    for g in range(3):
        near, far = 128 * g, 128 * (g + 3)
        first = even_in[32 * g : 32 * g + 25, :]
        second = odd_in[32 * g : 32 * g + 25, :]
        up = jnp.where(even, first, second)
        low = jnp.where(even, second, first)
        balance[near : near + 25, :] += jnp.where(lane < 64, low, 0.0)
        balance[far : far + 25, :] += jnp.where(lane < 64, pltpu.roll(low, 64, 1), 0.0)
        balance[near + 100 : near + 125, :] += jnp.where(lane >= 64, pltpu.roll(up, 64, 1), 0.0)
        balance[far + 100 : far + 125, :] += jnp.where(lane >= 64, up, 0.0)


def turn(values, slots):
    return values if slots % 8 == 0 else pltpu.roll(values, (16 * slots) % 128, 1)


def pack_lat(balance, side, even_out, odd_out):
    slot = lanes_of(5) // 16 % 4
    even = (side[0] & 1) == 0
    for g in range(2):
        for a in range(5):
            low = jnp.zeros((5, 128), f32)
            up = jnp.zeros((5, 128), f32)
            for t in range(4):
                j = 4 * g + t
                if j >= 6:
                    break
                base = 128 * j + 25 * a
                low = jnp.where(slot == t, turn(balance[base : base + 5, :], t), low)
                up = jnp.where(slot == t, turn(balance[base + 20 : base + 25, :], t - 3), up)
            at = 32 * g + 5 * a
            even_out[at : at + 5, :] = jnp.where(even, up, low)
            odd_out[at : at + 5, :] = jnp.where(even, low, up)


def add_lat(balance, side, even_in, odd_in):
    slot = lanes_of(5) // 16 % 4
    even = (side[0] & 1) == 0
    for g in range(2):
        for a in range(5):
            at = 32 * g + 5 * a
            first = even_in[at : at + 5, :]
            second = odd_in[at : at + 5, :]
            up = jnp.where(even, first, second)
            low = jnp.where(even, second, first)
            for t in range(4):
                j = 4 * g + t
                if j >= 6:
                    break
                base = 128 * j + 25 * a
                balance[base : base + 5, :] += jnp.where(slot == 0, turn(low, -t), 0.0)
                balance[base + 20 : base + 25, :] += jnp.where(slot == 3, turn(up, 3 - t), 0.0)


def middle_kernel(blk, lat, old, even_in, odd_in, balance, even_out, odd_out):
    balance[...] = old[...]
    add_cycle(balance, blk, even_in, odd_in)
    pack_lat(balance, lat, even_out, odd_out)


def advance(lat, old, even_in, odd_in, inverse, motion_in, speed_in, motion, speed, balance):
    balance[...] = old[...]
    add_lat(balance, lat, even_in, odd_in)
    scale = inverse[...]
    for j in range(6):
        part = slice(128 * j, 128 * j + 128)
        now = speed_in[part, :] + balance[part, :] * scale
        speed[part, :] = now
        motion[part, :] = motion_in[part, :] + now


def make_step_kernel(step):
    def step_kernel(
        blk,
        lat,
        old,
        even_in,
        odd_in,
        inverse,
        motion_in,
        speed_in,
        force,
        shear,
        lame,
        gradient,
        divergence,
        balance,
        motion,
        speed,
        integral,
        even_out,
        odd_out,
    ):
        advance(lat, old, even_in, odd_in, inverse, motion_in, speed_in, motion, speed, balance)
        balance_of(motion, force, step, shear, lame, gradient, divergence, balance, integral)
        pack_cycle(balance, blk, even_out, odd_out)

    return step_kernel


def scatter_to(table, state, points, groups):
    def point_rows(group):
        values = jnp.concatenate(
            [state[pl.ds(group * 8 + part, 16, stride=128), :] for part in range(8)], axis=0
        )
        start = group * 128
        points[pl.ds(start, 128), :] = values.T

    for group in groups:
        point_rows(group)
    part_of = lanes_of(1) // 16

    def point_places(a, b, c):
        point = 25 * a + 5 * b + c
        return lax.shift_right_logical(point, 3) * 128, part_of == (point & 7)

    def scatter_node(places, c, ex, ey, ez, node):
        del c
        at = places[0] + (64 * ex + 16 * ey + ez)
        table[pl.ds(node, 1), :] = jnp.where(places[1], points[pl.ds(at, 1), :], 0.0)

    return point_places, scatter_node


def state_of(balance, inverse, motion_in, speed_in, state):
    scale = inverse[...]
    for j in range(6):
        part = slice(128 * j, 128 * j + 128)
        now = speed_in[part, :] + balance[part, :] * scale
        state[768 + 128 * j : 896 + 128 * j, :] = now
        state[part, :] = motion_in[part, :] + now


def inner_kernel(
    numbers_hbm, balance, inverse, motion_in, speed_in, table, state, points, chunks, sems
):
    visit_pairs = start_pairs(numbers_hbm, chunks, sems, 3, INNER_PAIRS)
    state_of(balance, inverse, motion_in, speed_in, state)
    visit_pairs(*scatter_to(table, state, points, INNER_GROUPS))


def outer_kernel(
    numbers_hbm,
    balance,
    inverse,
    motion_in,
    speed_in,
    table_in,
    table,
    state,
    points,
    chunks,
    sems,
):
    del table_in
    visit_pairs = start_pairs(numbers_hbm, chunks, sems, 1, OUTER_PAIRS)
    state_of(balance, inverse, motion_in, speed_in, state)
    visit_pairs(*scatter_to(table, state, points, OUTER_GROUPS))


def last_kernel(
    numbers_hbm,
    lat,
    old,
    even_in,
    odd_in,
    inverse,
    motion_in,
    speed_in,
    table_in,
    motion_out,
    speed_out,
    table,
    balance,
    state,
    points,
    chunks,
    sems,
):
    del table_in
    visit_pairs = start_pairs(numbers_hbm, chunks, sems, 1, LAST_PAIRS)
    balance[...] = old[...]
    add_lat(balance, lat, even_in, odd_in)
    state_of(balance, inverse, motion_in, speed_in, state)
    visit_pairs(*scatter_to(table, state, points, LAST_GROUPS))

    def turned(start):
        values = table[pl.ds(start, 128), :].T
        total = values[0:16]
        for part in range(1, 8):
            total = total + values[16 * part : 16 * part + 16]
        return total

    def transpose_block(block):
        start = pl.multiple_of(block * 128, 128)
        values = turned(start)
        for q in range(3):
            motion_out[q, :, pl.ds(start, 128)] = values[2 * q : 2 * q + 2]
            speed_out[q, :, pl.ds(start, 128)] = values[6 + 2 * q : 8 + 2 * q]

    for_blocks(NODE_BLOCKS - 1, 7, transpose_block)
    start = 128 * (NODE_BLOCKS - 1)
    rest = NODES_DEV - start
    values = turned(start)
    for q in range(3):
        motion_out[q, :, start:NODES_DEV] = values[2 * q : 2 * q + 2, 0:rest]
        speed_out[q, :, start:NODES_DEV] = values[6 + 2 * q : 8 + 2 * q, 0:rest]


def spectrum_kernel(wide, first, second, third, fourth, out):
    values = jnp.concatenate([part[...] for part in (first, second, third, fourth)], axis=0)
    high, low = split2(values)
    zero = jnp.zeros((8, 128), bf16)
    out[...] = jnp.dot(
        wide[...], jnp.concatenate([high, low, high, zero], axis=0), preferred_element_type=f32
    )


def kept(*extent):
    return pltpu.VMEM(extent, f32)


def hold(*arrays):
    return tuple(pltpu.with_memory_space_constraint(array, pltpu.VMEM) for array in arrays)


def exchange(axis, odd, even, odd_pairs, even_pairs):
    odd = lax.ppermute(odd, axis, odd_pairs)
    even = lax.ppermute(even, axis, even_pairs)
    return odd, even


def chunk_scratch(pairs):
    return [pltpu.SMEM((640 * len(pairs),), jnp.int32), pltpu.SemaphoreType.DMA((len(pairs),))]


def limit(mebibytes):
    return pltpu.CompilerParams(vmem_limit_bytes=mebibytes * 1024 * 1024)


def local(
    displacement,
    velocity,
    lumped_mass,
    shear_modulus,
    lame_modulus,
    adjoint_sources,
    node_numbers,
    event_frequency,
):
    gradient, divergence, weight = (jnp.asarray(table) for table in operator_tables())
    pulses, wide = frequency_tables()
    blk = lax.axis_index("blk").astype(jnp.int32).reshape(1)
    lat = lax.axis_index("lat").astype(jnp.int32).reshape(1)
    numbers = node_numbers.reshape(125 * 128)
    blk_count = lax.axis_size("blk")
    lat_count = lax.axis_size("lat")
    cycle_even = [(i, i ^ 1) for i in range(blk_count)]
    cycle_odd = [(i, (((i + 1) ^ 1) - 1) % blk_count) for i in range(blk_count)]
    lat_even = [(i, i ^ 1) for i in range(lat_count)]
    lat_odd = [(i, ((i + 1) ^ 1) - 1) for i in range(1, lat_count - 1)]

    balance_shape, integral_shape = kept(768, 128), kept(10, 128)
    cycle_shape, lat_shape = kept(96, 128), kept(64, 128)
    (
        force,
        motion,
        speed,
        inverse,
        shear,
        lame,
        gradient,
        divergence,
        balance,
        integral,
        faces,
    ) = pl.pallas_call(
        gather_kernel,
        out_shape=(
            kept(24 * 128, 128),
            kept(768, 128),
            kept(768, 128),
            kept(128, 128),
            kept(128, 128),
            kept(128, 128),
            pltpu.VMEM((384, 384), bf16),
            pltpu.VMEM((128, 1152), bf16),
            balance_shape,
            integral_shape,
            kept(192, 128),
        ),
        in_specs=[hbm()] * 12 + [smem()],
        out_specs=[vmem()] * 11,
        scratch_shapes=[
            pltpu.VMEM((24, 3 * EVENTS), f32),
            pltpu.VMEM((COMPS, NODE_BLOCKS * 128), f32),
            pltpu.VMEM((NODE_BLOCKS * 128, 128), f32),
            *[pltpu.VMEM((NXN * 5 * LINE, 128), f32)] * 4,
            pltpu.VMEM((3, EVENTS, NODES_DEV), bf16),
            pltpu.VMEM((3, 2, NODES_DEV), f32),
            pltpu.VMEM((3, 2, NODES_DEV), f32),
            pltpu.VMEM((NODES_DEV,), f32),
            pltpu.VMEM((125, 128), f32),
            pltpu.VMEM((125, 128), f32),
            pltpu.VMEM((128, 128), f32),
            pltpu.VMEM((8, NFREQ), bf16),
            pltpu.VMEM((2, EVENTS), jnp.int32),
            pltpu.SemaphoreType.DMA((11,)),
            *chunk_scratch(MAIN_PAIRS),
            *chunk_scratch(FAR_PAIRS),
        ],
        compiler_params=limit(24),
        name="gather",
    )(
        *(
            pltpu.with_memory_space_constraint(array, pltpu.HBM)
            for array in (
                numbers,
                adjoint_sources.transpose(1, 0, 2),
                displacement.transpose(1, 0, 2),
                velocity.transpose(1, 0, 2),
                lumped_mass,
                shear_modulus,
                lame_modulus,
                weight,
                jnp.asarray(pulses),
                event_frequency,
                gradient,
                divergence,
            )
        ),
        blk,
    )
    force, motion, speed, inverse, shear, lame, gradient, divergence = hold(
        force, motion, speed, inverse, shear, lame, gradient, divergence
    )
    even, odd = faces[0:96], faces[96:192]
    integrals = []
    numbers_hbm = pltpu.with_memory_space_constraint(numbers, pltpu.HBM)
    table_shape = kept(NODE_BLOCKS * 128, 128)
    scatter_scratch = [pltpu.VMEM((2048, 128), f32), pltpu.VMEM((16 * 128, 128), f32)]
    for step in range(STEP_TOTAL):
        if step > 0:
            balance, motion, speed, integral, even, odd = pl.pallas_call(
                make_step_kernel(step),
                out_shape=(
                    balance_shape,
                    balance_shape,
                    balance_shape,
                    integral_shape,
                    cycle_shape,
                    cycle_shape,
                ),
                in_specs=[smem()] * 2 + [vmem()] * 11,
                out_specs=[vmem()] * 6,
                compiler_params=limit(8),
                name="step",
            )(
                blk,
                lat,
                balance,
                even,
                odd,
                inverse,
                motion,
                speed,
                force,
                shear,
                lame,
                gradient,
                divergence,
            )
            motion, speed = hold(motion, speed)
        integrals.append(integral)
        odd, even = exchange("blk", odd, even, cycle_odd, cycle_even)
        if step == STEP_TOTAL - 1:
            table = pl.pallas_call(
                inner_kernel,
                out_shape=table_shape,
                in_specs=[hbm()] + [vmem()] * 4,
                out_specs=vmem(),
                scratch_shapes=scatter_scratch + chunk_scratch(INNER_PAIRS),
                compiler_params=limit(16),
                name="inner",
            )(numbers_hbm, *hold(balance, inverse, motion, speed))
        balance, even, odd = pl.pallas_call(
            middle_kernel,
            out_shape=(balance_shape, lat_shape, lat_shape),
            in_specs=[smem()] * 2 + [vmem()] * 3,
            out_specs=[vmem()] * 3,
            compiler_params=limit(8),
            name="middle",
        )(blk, lat, *hold(balance, even, odd))
        odd, even = exchange("lat", odd, even, lat_odd, lat_even)
        balance, even, odd = hold(balance, even, odd)
    table = pl.pallas_call(
        outer_kernel,
        out_shape=table_shape,
        in_specs=[hbm()] + [vmem()] * 5,
        out_specs=vmem(),
        scratch_shapes=scatter_scratch + chunk_scratch(OUTER_PAIRS),
        input_output_aliases={5: 0},
        compiler_params=limit(16),
        name="outer",
    )(numbers_hbm, *hold(balance, inverse, motion, speed, table))
    spectrum = pl.pallas_call(
        spectrum_kernel,
        out_shape=jax.ShapeDtypeStruct((640, 128), f32),
        in_specs=[vmem()] * 5,
        out_specs=vmem(),
        compiler_params=limit(8),
        name="spectrum",
    )(*hold(jnp.asarray(wide), *integrals))
    nodal = jax.ShapeDtypeStruct((3, 2, NODES_DEV), f32)
    final_motion, final_speed, _ = pl.pallas_call(
        last_kernel,
        out_shape=(nodal, nodal, table_shape),
        in_specs=[hbm(), smem()] + [vmem()] * 7,
        out_specs=[vmem()] * 3,
        scratch_shapes=[pltpu.VMEM((768, 128), f32)] + scatter_scratch + chunk_scratch(LAST_PAIRS),
        input_output_aliases={8: 2},
        compiler_params=limit(16),
        name="last",
    )(
        numbers_hbm,
        lat,
        *hold(balance, even, odd, inverse, motion, speed, table),
    )
    return (
        final_motion.transpose(1, 0, 2),
        final_speed.transpose(1, 0, 2),
        spectrum.reshape(2, NFREQ, 5, 2, 128).transpose(0, 1, 3, 2, 4),
    )


def solution(mesh):
    nodes = P(None, None, ("blk", "lat"))
    columns = P(None, ("blk", "lat"))
    return jax.shard_map(
        local,
        mesh=mesh,
        in_specs=(nodes, nodes, P(("blk", "lat")), columns, columns, nodes, columns, P()),
        out_specs=(nodes, nodes, P(None, None, None, None, ("blk", "lat"))),
        check_vma=False,
    )
```
